512 devices in a mesh: ctx: 64 (over z_lo, x, core), tp: 8 (over y, z_hi).
Axes of the slice: x: 4, y: 4, z: 16 (z_hi: 2, z_lo: 8; z = z_hi * 8 + z_lo), core: 2. Of those that a mesh axis runs over, the one named last changes fastest.
Arguments:
- stored: bfloat16 [8192, 4096], P('ctx', 'tp'), may hold values from -6 to 6
- source_owner: int32 [8192], P('ctx'), may hold values from 0 to 63, as said below
- doc_ids: int32 [8192], P('ctx'), may hold values from 0 to 48, as said below
- doc_starts: int32 [49], replicated, may hold values from 0 to 8184, as said below
- wq: bfloat16 [4096, 4096], P('ctx', 'tp'), may hold values from -1 to 1
- wk: bfloat16 [4096, 1024], P('ctx', 'tp'), may hold values from -1 to 1
- wv: bfloat16 [4096, 1024], P('ctx', 'tp'), may hold values from -0.09375 to 0.09375
Outputs:
- context: bfloat16 [8192, 4096], P('ctx', 'tp')
The draws below stay inside these ranges and needn't reach their ends.
Inputs may be any that keep to these rules, and one draw needn't show every extreme that they name: `source_owner`: every owner stores exactly 128 rows, taken in packed order; each packed shard of 128 rows takes at most 4 rows from any one owner, and exactly 4 from some owner. `doc_ids`: Nondecreasing; document k occupies positions doc_starts[k] up to the next document's start; one document has exactly 5120 tokens. Increasing, doc_starts[0] = 0, consistent with doc_ids.
All inputs are finite; a program needn't handle non-finite values.
Results may differ from the reference program's by a relative error of at most 0.0035.
The reference program's roundings to bfloat16 on the way (of `packed` and `queries`) count: a program that leaves them out, or rounds other values in their place, can miss the bound.
Values may be sent and summed in bfloat16 or wider, within the bound.
A program may use at most 64 MiB of HBM per device.

```python
import math
import jax
import jax.numpy as jnp
from jax import lax

MODEL_WIDTH = 4096
QUERY_HEADS = 32
KEY_VALUE_HEADS = 8
HEAD_SIZE = 128
DOC_MEAN = 64
TOK_DEV = 128
WINDOW_TOKENS = 8192
MOST = 5120
NDOC = 49
N_CTX = 64


def draw_source_owner(key, part):
    mean = TOK_DEV // N_CTX
    key_spread, key_order, key_owner = jax.random.split(jax.random.fold_in(key, 11), 3)
    spread = jax.random.randint(key_spread, (N_CTX // 2,), 0, mean + 1).astype(jnp.int32)
    spread = spread.at[0].set(mean)
    amounts = jnp.concatenate([mean + spread, mean - spread]).astype(jnp.int32)
    shifts = jnp.repeat(jnp.arange(N_CTX, dtype=jnp.int32), amounts, total_repeat_length=TOK_DEV)
    block_keys = jax.random.split(key_order, N_CTX)

    def shuffle(block_key):
        return jax.random.permutation(block_key, shifts)
    shuffled = jax.vmap(shuffle)(block_keys)
    relabel = jax.random.permutation(key_owner, N_CTX).astype(jnp.int32)
    blocks = jnp.arange(N_CTX, dtype=jnp.int32)[:, None]
    return relabel[(blocks + shuffled) % N_CTX].reshape(WINDOW_TOKENS).astype(jnp.int32)


def document_plan(key):
    shorts = NDOC - 1
    key_spread, key_order = jax.random.split(jax.random.fold_in(key, 23))
    spread = jax.random.randint(key_spread, (shorts // 2,), 0, DOC_MEAN - 7).astype(jnp.int32)
    lengths = jnp.concatenate([jnp.full((1,), MOST, jnp.int32), DOC_MEAN + spread, DOC_MEAN - spread])
    lengths = lengths[jax.random.permutation(key_order, NDOC)]
    return (jnp.cumsum(lengths) - lengths).astype(jnp.int32)


def draw_doc_starts(key, part):
    return document_plan(key)


def draw_doc_ids(key, part):
    starts = document_plan(key)
    places = jnp.arange(WINDOW_TOKENS, dtype=jnp.int32)
    inside = (starts[None, :] <= places[:, None]).astype(jnp.int32)
    return (jnp.sum(inside, axis=1) - 1).astype(jnp.int32)


def projection_pair(key):
    key_query, key_from_keys = jax.random.split(jax.random.fold_in(key, 31))
    key_matrix = jax.random.normal(key_from_keys, (MODEL_WIDTH, KEY_VALUE_HEADS * HEAD_SIZE), jnp.float32) / math.sqrt(MODEL_WIDTH)
    noise = jax.random.normal(key_query, (MODEL_WIDTH, QUERY_HEADS * HEAD_SIZE), jnp.float32) / math.sqrt(MODEL_WIDTH)
    query_w = 3.0 * noise
    return (jnp.clip(query_w, -1.0, 1.0), jnp.clip(key_matrix, -1.0, 1.0))


def draw_wq(key, part):
    return projection_pair(key)[0].astype(jnp.bfloat16)


def draw_wk(key, part):
    return projection_pair(key)[1].astype(jnp.bfloat16)


def levels(own_key, extent, cuts, least, largest):
    gain, own = 1.0, jax.random.fold_in(own_key, 6)
    for axis_at, parts in cuts:
        steps = jnp.exp(jax.random.uniform(jax.random.fold_in(own, axis_at), (parts,), jnp.float32, least / len(cuts), largest / len(cuts)))
        gain = gain * jnp.repeat(steps, extent[axis_at] // parts).reshape([-1 if axis == axis_at else 1 for axis in range(len(extent))])
    return gain


def centred(own_key, dims, scale, bound, cuts=(), held_as=jnp.bfloat16):
    entries = scale * jax.random.normal(own_key, dims, jnp.float32)
    if cuts:
        entries = entries * levels(own_key, dims, cuts, -0.22, 0.18)
    return jnp.clip(entries, -bound, bound).astype(held_as)


def setup_inputs(seed: int = 0) -> dict:
    keys = jax.random.split(jax.random.key(seed), 8)
    stored = centred(keys[0], (WINDOW_TOKENS, MODEL_WIDTH), 1.0, 6.0, ((0, 64), (1, 8)))
    source_owner = draw_source_owner(jax.random.fold_in(keys[7], 71), 0)
    doc_ids = draw_doc_ids(jax.random.fold_in(keys[7], 71), 0)
    doc_starts = draw_doc_starts(jax.random.fold_in(keys[7], 71), 0)
    wq = draw_wq(jax.random.fold_in(keys[7], 71), 0)
    wk = draw_wk(jax.random.fold_in(keys[7], 71), 0)
    wv = centred(keys[6], (MODEL_WIDTH, KEY_VALUE_HEADS * HEAD_SIZE), MODEL_WIDTH ** -0.5, 0.09375, ((0, 64), (1, 8)))
    return {"stored": stored, "source_owner": source_owner, "doc_ids": doc_ids, "doc_starts": doc_starts, "wq": wq, "wk": wk, "wv": wv}


rope_base = 500000.0


def apply_rotary(value_rows, token_positions, heads):
    rows = value_rows.shape[0]
    size = value_rows.shape[1] // heads
    half = size // 2
    freqs = rope_base ** (-jnp.arange(half, dtype=jnp.float32) * 2.0 / size)
    angles = token_positions.astype(jnp.float32)[:, None] * freqs[None, :]
    cosine = jnp.cos(angles)[:, None, :]
    sine = jnp.sin(angles)[:, None, :]
    shaped = value_rows.reshape(rows, heads, size)
    first = shaped[..., :half]
    second = shaped[..., half:]
    joined = jnp.concatenate([first * cosine - second * sine, second * cosine + first * sine], axis=-1)
    return joined.reshape(rows, heads * size)


def reference(stored, source_owner, doc_ids, doc_starts, wq, wk, wv):
    owners_hot = (source_owner[:, None] == jnp.arange(N_CTX, dtype=jnp.int32)[None, :]).astype(jnp.int32)
    earlier = jnp.cumsum(owners_hot, axis=0).astype(jnp.int32) - owners_hot
    rank = jnp.sum(earlier * owners_hot, axis=1).astype(jnp.int32)
    packed = stored[(source_owner * TOK_DEV + rank).astype(jnp.int32)]
    queries_raw = jnp.dot(packed, wq, preferred_element_type=jnp.float32)
    unrotated_keys = jnp.dot(packed, wk, preferred_element_type=jnp.float32)
    values_raw = jnp.dot(packed, wv, preferred_element_type=jnp.float32)
    token_positions = (jnp.arange(WINDOW_TOKENS, dtype=jnp.int32) - doc_starts[doc_ids]).astype(jnp.int32)
    queries = apply_rotary(queries_raw, token_positions, QUERY_HEADS).astype(jnp.bfloat16)
    key_rows = apply_rotary(unrotated_keys, token_positions, KEY_VALUE_HEADS).astype(jnp.bfloat16)
    value_rows = values_raw.astype(jnp.bfloat16)
    query_group = QUERY_HEADS // KEY_VALUE_HEADS
    rows_per_block = 128
    scale = 1.0 / (HEAD_SIZE ** 0.5)
    every_key_row = key_rows.astype(jnp.float32).reshape(WINDOW_TOKENS, KEY_VALUE_HEADS, HEAD_SIZE)
    every_value_row = value_rows.astype(jnp.float32).reshape(WINDOW_TOKENS, KEY_VALUE_HEADS, HEAD_SIZE)

    def block(index):
        start = (index * rows_per_block).astype(jnp.int32)
        query_block = lax.dynamic_slice_in_dim(queries, start, rows_per_block, 0).astype(jnp.float32)
        query_block = query_block.reshape(rows_per_block, KEY_VALUE_HEADS, query_group, HEAD_SIZE)
        ids_blk = lax.dynamic_slice_in_dim(doc_ids, start, rows_per_block, 0)
        scores = jnp.einsum("qhgd,khd->hgqk", query_block, every_key_row) * scale
        same = (ids_blk[:, None] == doc_ids[None, :])[None, None]
        top = jnp.max(jnp.where(same, scores, -1e30), axis=-1)
        weights = jnp.where(same, jnp.exp(scores - top[..., None]), 0.0)
        total = jnp.sum(weights, axis=-1)
        rounded = lax.optimization_barrier(weights.astype(jnp.bfloat16)).astype(jnp.float32)
        mixed = jnp.einsum("hgqk,khd->qhgd", rounded, every_value_row)
        result = mixed / jnp.transpose(total, (2, 0, 1))[..., None]
        return result.reshape(rows_per_block, QUERY_HEADS * HEAD_SIZE).astype(jnp.bfloat16)

    blocks = lax.map(block, jnp.arange(WINDOW_TOKENS // rows_per_block, dtype=jnp.int32))
    return blocks.reshape(WINDOW_TOKENS, QUERY_HEADS * HEAD_SIZE)
```

```python
import functools

import jax
import jax.numpy as jnp
from jax import lax
from jax.experimental import pallas as pl
from jax.experimental.pallas import tpu as pltpu
from jax.sharding import PartitionSpec as P

HEAD = 128
ROPE_BASE = 500000.0
MESH = pl.DeviceIdType.MESH
F32 = jnp.float32
BF16 = jnp.bfloat16
NZ, NX = 8, 4
NCTX = 64
CAP = 4
WB = 384
KB = 272
LAG = 2
ACT = 5
OFF = 6


def dot(a, b):
    return jnp.dot(a, b, preferred_element_type=F32)


def iota(shape, dim):
    return lax.broadcasted_iota(jnp.int32, shape, dim)


def plane_at(z, i):
    low = jnp.minimum(z, NZ - 1 - z)
    near = (i + 1) // 2
    both = jnp.where(i % 2 == 1, z - near, z + near)
    one = jnp.where(z < NZ // 2, z + (i - low), z - (i - low))
    return jnp.where(i <= 2 * low, both, one)


class Gather:
    def __init__(self, buf, chunks, zs, zr, xs, xr, fs, fr, place):
        self.buf, self.chunks = buf, chunks
        self.zs, self.zr, self.xs, self.xr, self.fs, self.fr = zs, zr, xs, xr, fs, fr
        self.z, self.x, self.core = place

    def part(self, plane, x, q):
        start, size = self.chunks[q]
        return self.buf.at[plane, x, pl.ds(start, size)]

    def copy(self, plane, x, q, send, recv, z, to_x):
        ref = self.part(plane, x, q)
        return pltpu.make_async_remote_copy(
            src_ref=ref,
            dst_ref=ref,
            send_sem=send,
            recv_sem=recv,
            device_id={"ctx": z * 8 + to_x * 2 + self.core},
            device_id_type=MESH,
        )

    def along_z(self, plane, q, step):
        k = 0 if step > 0 else 1
        return self.copy(
            plane, self.x, q, self.zs.at[plane, q, k], self.zr.at[plane, q], self.z + step, self.x
        )

    def along_x(self, plane, q, k):
        to_x = (self.x + (1 if k == 0 else 3)) % NX
        return self.copy(
            plane, self.x, q, self.xs.at[plane, q, k], self.xr.at[plane, q, k], self.z, to_x
        )

    def came_x(self, plane, q, k):
        from_x = (self.x + (3 if k == 0 else 1)) % NX
        return self.copy(
            plane, from_x, q, self.xs.at[plane, q, k], self.xr.at[plane, q, k], self.z, from_x
        )

    def onward(self, plane, k):
        block_x = (self.x + (3 if k == 0 else 1)) % NX
        to_x = (self.x + (1 if k == 0 else 3)) % NX
        return self.copy(
            plane, block_x, k, self.fs.at[plane, k], self.fr.at[plane, k], self.z, to_x
        )

    def came_onward(self, plane, k):
        far_x = (self.x + 2) % NX
        return self.copy(
            plane, far_x, k, self.fs.at[plane, k], self.fr.at[plane, k], self.z, far_x
        )

    def spread(self, plane, q):
        @pl.when((plane <= self.z) & (self.z < NZ - 1))
        def _():
            self.along_z(plane, q, 1).start()

        @pl.when((plane >= self.z) & (self.z > 0))
        def _():
            self.along_z(plane, q, -1).start()

        self.along_x(plane, q, 0).start()
        self.along_x(plane, q, 1).start()

    def arrive(self, plane):
        for q in range(2):
            self.along_z_wait(plane, q)
            self.spread(plane, q)

    def along_z_wait(self, plane, q):
        self.copy(
            plane, self.x, q, self.zs.at[plane, q, 0], self.zr.at[plane, q], self.z, self.x
        ).wait_recv()

    def pass_on(self, plane):
        for k in range(2):
            self.came_x(plane, k, k).wait_recv()
            self.onward(plane, k).start()

    def complete(self, plane):
        self.came_x(plane, 1, 0).wait_recv()
        self.came_x(plane, 0, 1).wait_recv()
        self.came_onward(plane, 0).wait_recv()
        self.came_onward(plane, 1).wait_recv()

    def drain(self):
        @pl.loop(0, NZ)
        def _(plane):
            for q in range(2):

                @pl.when((plane <= self.z) & (self.z < NZ - 1))
                def _():
                    self.along_z(plane, q, 1).wait_send()

                @pl.when((plane >= self.z) & (self.z > 0))
                def _():
                    self.along_z(plane, q, -1).wait_send()

                self.along_x(plane, q, 0).wait_send()
                self.along_x(plane, q, 1).wait_send()
                self.onward(plane, q).wait_send()


def kernel(
    stored, owner_ref, doc_ref, starts_ref, freq_ref, wq, wk, wv, out,
    meta, table, swap, wg, xa, acc, cosine, sine, select, unpack, pos_doc, q_doc,
    outgoing, incoming, kv, qp, top, total, summed,
    table_send, table_recv, swap_sems, act_send, act_recv,
    wzs, wzr, wxs, wxr, wfs, wfr,
    kzs, kzr, kxs, kxr, kfs, kfr,
    sib_send, sib_recv, q_send, q_recv,
):
    c = lax.axis_index("ctx")
    t = lax.axis_index("tp")
    z, x, core = c // 8, (c // 2) % NX, c % 2
    y, zh = t // 2, t % 2
    chip = c // 2
    sib = chip * 2 + (1 - core)
    place = (z, x, core)

    barrier = pltpu.get_barrier_semaphore()

    @pl.loop(1, NCTX)
    def _(i):
        pl.semaphore_signal(
            barrier, inc=1, device_id={"ctx": (c + i) % NCTX}, device_id_type=MESH
        )

    def y_peer(step):
        return ((y + step) % 4) * 2 + zh

    twin = y * 2 + (1 - zh)
    for to in (y_peer(1), y_peer(2), y_peer(3), twin):
        pl.semaphore_signal(barrier, inc=1, device_id={"tp": to}, device_id_type=MESH)
    pl.semaphore_wait(barrier, NCTX - 1 + 4)

    weights = Gather(wg, ((0, 192), (192, 192)), wzs, wzr, wxs, wxr, wfs, wfr, place)
    keyvals = Gather(kv.at[core], ((0, 144), (144, 128)), kzs, kzr, kxs, kxr, kfs, kfr, place)

    first = core == 0
    for g in range(3):
        if g < 2:
            low = wq[:, g * HEAD : (g + 1) * HEAD]
            high = wq[:, (g + 2) * HEAD : (g + 3) * HEAD]
        else:
            low, high = wk[...], wv[...]
        mine = jnp.where(first, low, high)
        other = jnp.where(first, high, low)
        swap[g * 64 : (g + 1) * 64, :] = other
        wg[z, x, pl.ds(pl.multiple_of(core * 192 + g * 64, 64), 64), :] = mine
    half = wg.at[z, x, pl.ds(pl.multiple_of(core * 192, 64), 192)]
    swapping = pltpu.make_async_remote_copy(
        src_ref=swap,
        dst_ref=half,
        send_sem=swap_sems.at[0],
        recv_sem=swap_sems.at[1],
        device_id={"ctx": sib},
        device_id_type=MESH,
    )
    swapping.start()

    @pl.when(first)
    def _():
        weights.spread(z, 0)

    @pl.when(jnp.logical_not(first))
    def _():
        weights.spread(z, 1)

    def act(src, slot, k, axis, to):
        return pltpu.make_async_remote_copy(
            src_ref=src,
            dst_ref=xa.at[slot, core],
            send_sem=act_send.at[k],
            recv_sem=act_recv.at[slot, core],
            device_id={axis: to},
            device_id_type=MESH,
        )

    def act_wait(slot, who):
        pltpu.make_async_remote_copy(
            src_ref=xa.at[slot, who],
            dst_ref=xa.at[slot, who],
            send_sem=act_send.at[0],
            recv_sem=act_recv.at[slot, who],
            device_id={"tp": t},
            device_id_type=MESH,
        ).wait_recv()

    own_acts = [act(stored, t, 0, "tp", twin)]
    own_acts += [act(stored, t, k, "tp", y_peer(k)) for k in (1, 3, 2)]
    own_acts += [act(stored, t, 4, "ctx", sib)]
    for one in own_acts:
        one.start()
    twin_acts = [act(xa.at[twin, core], twin, 4 + k, "tp", y_peer(k)) for k in (1, 3, 2)]
    twin_acts += [act(xa.at[twin, core], twin, 8, "ctx", sib)]
    across = [
        act(xa.at[y_peer(k), core], y_peer(k), 8 + k, "ctx", sib) for k in (1, 2, 3)
    ]
    across_twin = [
        act(xa.at[(y_peer(k) // 2) * 2 + (1 - zh), core], (y_peer(k) // 2) * 2 + (1 - zh), 11 + k, "ctx", sib)
        for k in (1, 2, 3)
    ]

    xa[t, core] = stored[...]

    pltpu.make_async_remote_copy(
        src_ref=swap,
        dst_ref=wg.at[z, x, pl.ds(pl.multiple_of((1 - core) * 192, 64), 192)],
        send_sem=swap_sems.at[0],
        recv_sem=swap_sems.at[1],
        device_id={"ctx": sib},
        device_id_type=MESH,
    ).wait_recv()

    @pl.when(first)
    def _():
        weights.spread(z, 1)

    @pl.when(jnp.logical_not(first))
    def _():
        weights.spread(z, 0)

    meta[0:1, :] = owner_ref[...]
    meta[1:2, :] = doc_ref[...]

    def table_copy(to):
        return pltpu.make_async_remote_copy(
            src_ref=meta,
            dst_ref=table.at[c],
            send_sem=table_send,
            recv_sem=table_recv,
            device_id={"ctx": to},
            device_id_type=MESH,
        )

    @pl.loop(1, NCTX)
    def _(i):
        table_copy((c + i) % NCTX).start()

    own_row = pltpu.make_async_copy(meta, table.at[c], table_recv)
    own_row.start()

    def plan():
        pltpu.make_async_copy(table, table, table_recv).wait()
        owners = table[:, 0, :]
        docs = table[:, 1, :].astype(F32).astype(BF16)
        before_l = (iota((128, 128), 0) < iota((128, 128), 1)).astype(F32).astype(BF16)
        before_s = (iota((64, 64), 1) < iota((64, 64), 0)).astype(F32).astype(BF16)
        rows = iota((512, 128), 0)
        spread_rows = (iota((512, 64), 0) // 8 == iota((512, 64), 1)).astype(F32).astype(BF16)
        doc_tile = jnp.zeros((16, 128), F32)
        for oc in range(2):
            hit = owners == chip * 2 + oc
            hot = hit.astype(F32)
            hot16 = hot.astype(BF16)
            lane_before = dot(hot16, before_l)
            count = jnp.broadcast_to(jnp.sum(hot, axis=1, keepdims=True), (64, 128))
            before = jnp.broadcast_to(
                jnp.sum(dot(before_s, hot16), axis=1, keepdims=True), (64, 128)
            )
            rank1 = jnp.where(hit, before + lane_before + 1.0, 0.0)
            before_t = jnp.concatenate([before, before], axis=0).T[:, :64]
            count_t = jnp.concatenate([count, count], axis=0).T[:, :64]
            r64 = iota((128, 64), 0).astype(F32)
            shard_hot = jnp.where((before_t <= r64) & (r64 < before_t + count_t), 1.0, 0.0)
            shard_hot16 = shard_hot.astype(BF16)
            ranks = dot(shard_hot16, rank1.astype(BF16))
            found = ranks == iota((128, 128), 0).astype(F32) + 1.0
            lane = jnp.sum(
                jnp.where(found, iota((128, 128), 1).astype(F32), 0.0), axis=1, keepdims=True
            )
            doc = jnp.sum(
                jnp.where(found, dot(shard_hot16, docs), 0.0), axis=1, keepdims=True
            )
            shard = jnp.sum(
                shard_hot * iota((128, 64), 1).astype(F32), axis=1, keepdims=True
            )
            n_doc = starts_ref.shape[1]
            starts = jnp.broadcast_to(starts_ref[...].astype(F32), (128, n_doc))
            start = jnp.sum(
                jnp.where(doc == iota((128, n_doc), 1).astype(F32), starts, 0.0),
                axis=1,
                keepdims=True,
            )
            position = shard * 128.0 + lane - start
            angle = position * freq_ref[...]
            span = pl.ds(oc * 128, 128)
            cosine[span, :] = jnp.cos(angle)
            sign = jnp.where(iota((128, 128), 1) < 64, -1.0, 1.0)
            sine[span, :] = jnp.sin(angle) * sign
            doc_rows = jnp.broadcast_to(doc, (128, 128)).T
            doc_tile = jnp.where(iota((16, 128), 0) == oc, doc_rows[:16], doc_tile)
            begin = dot(spread_rows, before.astype(BF16))
            many = dot(spread_rows, count.astype(BF16))
            slot = (rows % CAP).astype(F32)
            chosen = (
                (iota((512, 128), 1).astype(F32) == begin + slot)
                & (slot < many)
                & ((rows // CAP) % 2 == oc)
            )
            select[:, oc * 128 : (oc + 1) * 128] = jnp.where(chosen, 1.0, 0.0).astype(BF16)
        pos_doc[...] = doc_tile.astype(BF16)
        mine = jnp.broadcast_to(owner_ref[...].astype(F32), (128, 128))
        mine_t = mine.T
        same = (mine == mine_t) & (iota((128, 128), 1) < iota((128, 128), 0))
        order = jnp.sum(jnp.where(same, 1.0, 0.0), axis=1, keepdims=True)
        col = iota((128, 512), 1)
        owner_col = ((col // 16) * 2 + (col // CAP) % 2).astype(F32)
        slot_col = (col % CAP).astype(F32)
        mine_col = jnp.broadcast_to(mine_t[:, :1], (128, 512))
        for hd in range(2):
            pick = (owner_col == mine_col) & (slot_col == order) & ((col // 8) % 2 == hd)
            unpack[hd] = jnp.where(pick, 1.0, 0.0).astype(BF16)
        q_doc[...] = jnp.broadcast_to(doc_ref[...].astype(F32), (128, 128)).T

    def project(plane):
        columns = []
        for xx in range(NX):
            for half_core in range(2):
                tiles = [
                    wg[plane, xx, half_core * 192 + g * 64 : half_core * 192 + (g + 1) * 64, :]
                    for g in range(3)
                ]
                columns.append(jnp.concatenate(tiles, axis=1))
        w = jnp.concatenate(columns, axis=0)
        acts = xa[plane].reshape(256, 512)
        acc[...] += dot(acts, w)

    acc[...] = jnp.zeros_like(acc)

    @pl.loop(0, NZ + OFF)
    def _(i):
        @pl.when((i > 0) & (i < NZ))
        def _():
            weights.arrive(plane_at(z, i))

        @pl.when(i == 1)
        def _():
            for k in (1, 2, 3):
                act_wait(y_peer(k), core)
                across[k - 1].start()

        @pl.when(i == 2)
        def _():
            plan()

        @pl.when(i == 3)
        def _():
            act_wait(twin, core)
            for one in twin_acts:
                one.start()

        @pl.when(i == ACT)
        def _():
            for k in (1, 2, 3):
                act_wait((y_peer(k) // 2) * 2 + (1 - zh), core)
                across_twin[k - 1].start()

        @pl.when((i >= LAG) & (i < NZ + LAG))
        def _():
            weights.pass_on(plane_at(z, i - LAG))

        @pl.when(i == OFF)
        def _():
            @pl.loop(0, 8)
            def _(slot):
                act_wait(slot, 1 - core)

        @pl.when(i >= OFF)
        def _():
            plane = plane_at(z, i - OFF)
            weights.complete(plane)
            project(plane)

    def rotate(v):
        return v * cosine[...] + pltpu.roll(v, 64, 1) * sine[...]

    third = acc[:, 256:384]
    kv[core, z, x, 0:256, :] = jnp.where(first, rotate(third), third).astype(BF16)
    kv[core, z, x, 256:272, :] = pos_doc[...]
    keyvals.spread(z, 0)
    keyvals.spread(z, 1)
    blocks = []
    for hd in range(2):
        rotated = rotate(acc[:, hd * HEAD : (hd + 1) * HEAD]).astype(BF16)
        blocks.append(dot(select[...], rotated).reshape(64, 8, HEAD))
    outgoing[...] = jnp.concatenate(blocks, axis=1).astype(BF16)

    def q_copy(to):
        return pltpu.make_async_remote_copy(
            src_ref=outgoing.at[to],
            dst_ref=incoming.at[core, chip],
            send_sem=q_send,
            recv_sem=q_recv,
            device_id={"ctx": to},
            device_id_type=MESH,
        )

    @pl.loop(1, NCTX)
    def _(i):
        q_copy((c + i) % NCTX).start()

    pltpu.make_async_copy(outgoing.at[c], incoming.at[core, chip], q_recv).start()

    def sibling(plane, who):
        return pltpu.make_async_remote_copy(
            src_ref=kv.at[who, plane],
            dst_ref=kv.at[who, plane],
            send_sem=sib_send.at[plane],
            recv_sem=sib_recv.at[plane],
            device_id={"ctx": sib},
            device_id_type=MESH,
        )

    top[...] = jnp.full_like(top, -1e30)
    total[...] = jnp.zeros_like(total)
    summed[...] = jnp.zeros_like(summed)
    factor2 = 1.4426950408889634 / HEAD**0.5

    def collect():
        pltpu.make_async_copy(incoming, incoming, q_recv).wait()
        for who in range(2):
            block = incoming[who].reshape(512, HEAD)
            for hd in range(2):
                qp[who * 2 + hd] = dot(unpack[hd], block).astype(BF16)

    def attend(plane):
        ids = []
        for xx in range(NX):
            tile = kv[0, plane, xx, 256:272, :].astype(F32)
            ids += [tile[0:1, :], tile[1:2, :]]
        key_doc = jnp.concatenate(ids, axis=1)
        qd = jnp.concatenate([q_doc[...]] * 8, axis=1)
        kept = qd == key_doc

        @pl.loop(0, 4)
        def _(h):
            q = qp[h]
            parts = [
                lax.dot_general(
                    q,
                    kv[0, plane, xx, 0:256, :],
                    (((1,), (1,)), ((), ())),
                    preferred_element_type=F32,
                )
                for xx in range(NX)
            ]
            scores = jnp.concatenate(parts, axis=1)
            scores = jnp.where(kept, scores * factor2, -2e30)
            old = top[h]
            new = jnp.maximum(old, jnp.max(scores, axis=1, keepdims=True))
            weights_ = jnp.exp2(scores - new[:, :1])
            fall = jnp.exp2(old - new)
            total[h] = total[h] * fall + jnp.sum(weights_, axis=1, keepdims=True)
            rounded = weights_.astype(BF16)
            mixed = dot(rounded[:, 0:256], kv[1, plane, 0, 0:256, :])
            for xx in range(1, NX):
                mixed += dot(rounded[:, xx * 256 : (xx + 1) * 256], kv[1, plane, xx, 0:256, :])
            summed[h] = summed[h] * fall + mixed
            top[h] = new

    @pl.loop(0, NZ + 3)
    def _(i):
        @pl.when((i > 0) & (i < NZ))
        def _():
            keyvals.arrive(plane_at(z, i))

        @pl.when((i >= 1) & (i < NZ + 1))
        def _():
            keyvals.pass_on(plane_at(z, i - 1))

        @pl.when((i >= 2) & (i < NZ + 2))
        def _():
            plane = plane_at(z, i - 2)
            keyvals.complete(plane)
            sibling(plane, core).start()

        @pl.when(i == 3)
        def _():
            collect()

        @pl.when(i >= 3)
        def _():
            plane = plane_at(z, i - 3)
            sibling(plane, 1 - core).wait_recv()
            attend(plane)

    for h in range(4):
        out[:, h * HEAD : (h + 1) * HEAD] = (summed[h] / total[h]).astype(BF16)

    swapping.wait_send()
    for one in own_acts + twin_acts + across + across_twin:
        one.wait_send()
    weights.drain()
    keyvals.drain()

    @pl.loop(0, NZ)
    def _(plane):
        sibling(plane, core).wait_send()

    pltpu.make_async_copy(table.at[pl.ds(0, 63)], table.at[pl.ds(0, 63)], table_send).wait()
    pltpu.make_async_copy(
        outgoing.at[pl.ds(0, 63)], outgoing.at[pl.ds(0, 63)], q_send
    ).wait()


def body(stored, source_owner, doc_ids, doc_starts, wq, wk, wv):
    half = HEAD // 2
    freqs = ROPE_BASE ** (-jnp.arange(half, dtype=F32) * 2.0 / HEAD)
    freqs = jnp.concatenate([freqs, freqs])[None, :]
    dma = pltpu.SemaphoreType.DMA
    ring_sems = [
        dma((NZ, 2, 2)), dma((NZ, 2)), dma((NZ, 2, 2)), dma((NZ, 2, 2)), dma((NZ, 2)), dma((NZ, 2)),
    ]
    scratch = [
        pltpu.VMEM((2, 128), jnp.int32),
        pltpu.VMEM((NCTX, 2, 128), jnp.int32),
        pltpu.VMEM((192, HEAD), BF16),
        pltpu.VMEM((NZ, NX, WB, HEAD), BF16),
        pltpu.VMEM((8, 2, 128, 512), BF16),
        pltpu.VMEM((256, 384), F32),
        pltpu.VMEM((256, HEAD), F32),
        pltpu.VMEM((256, HEAD), F32),
        pltpu.VMEM((512, 256), BF16),
        pltpu.VMEM((2, 128, 512), BF16),
        pltpu.VMEM((16, 128), BF16),
        pltpu.VMEM((128, 128), F32),
        pltpu.VMEM((NCTX, 16, HEAD), BF16),
        pltpu.VMEM((2, NCTX // 2, 16, HEAD), BF16),
        pltpu.VMEM((2, NZ, NX, KB, HEAD), BF16),
        pltpu.VMEM((4, 128, HEAD), BF16),
        pltpu.VMEM((4, 128, HEAD), F32),
        pltpu.VMEM((4, 128, HEAD), F32),
        pltpu.VMEM((4, 128, HEAD), F32),
        dma, dma, dma((2,)), dma((15,)), dma((8, 2)),
        *ring_sems,
        *ring_sems,
        dma((NZ,)), dma((NZ,)), dma, dma,
    ]
    vmem = pl.BlockSpec(memory_space=pltpu.VMEM)
    return pl.pallas_call(
        kernel,
        out_shape=jax.ShapeDtypeStruct((128, 512), BF16),
        in_specs=[vmem] * 8,
        out_specs=vmem,
        scratch_shapes=scratch,
        compiler_params=pltpu.CompilerParams(
            collective_id=0, has_side_effects=True, vmem_limit_bytes=48 << 20
        ),
        name="layer",
    )(stored, source_owner[None, :], doc_ids[None, :], doc_starts[None, :], freqs, wq, wk, wv)


def solution(mesh):
    return jax.shard_map(
        body,
        mesh=mesh,
        in_specs=(
            P("ctx", "tp"), P("ctx"), P("ctx"), P(), P("ctx", "tp"), P("ctx", "tp"), P("ctx", "tp"),
        ),
        out_specs=P("ctx", "tp"),
        check_vma=False,
    )
```

```python
import functools

import jax
import jax.numpy as jnp
import numpy as np
from jax import lax
from jax.experimental import pallas as pl
from jax.experimental.pallas import tpu as pltpu
from jax.sharding import PartitionSpec as P

HEAD = 128
ROPE_BASE = 500000.0
MESH = pl.DeviceIdType.MESH
F32 = jnp.float32
BF16 = jnp.bfloat16
NZ, NX = 8, 4
NCTX = 64
CAP = 4
WB = 384
KB = 272
NQ = 2
KQ = 2
NEAR = (2, 3, 5, 7)
PLAN = (4, 5, 7, 8)
TWIN = (5, 6, 8, 8)
FAR = (7, 8, 9, 9)
WPASS = (1, 2, 4, 6)
WDONE = (10, 10, 10, 10)
KPASS = (1, 2, 4, 6)
KDONE = (2, 3, 5, 7)
QMID = (3, 4, 7, 8)
QGOT = (5, 6, 9, 10)
ATT = (5, 6, 9, 10)
ORDER = (
    (0, 1, 2, 3, 4, 5, 6, 7),
    (1, 0, 2, 3, 4, 5, 6, 7),
    (2, 3, 1, 4, 0, 5, 6, 7),
    (3, 4, 2, 5, 1, 6, 7, 0),
)


def dot(a, b):
    return jnp.dot(a, b, preferred_element_type=F32)


def iota(shape, dim):
    return lax.broadcasted_iota(jnp.int32, shape, dim)


def plane_at(z, i):
    low = jnp.minimum(z, NZ - 1 - z)
    packed = [sum(p << (3 * n) for n, p in enumerate(row)) for row in ORDER]
    code = jnp.where(
        low < 2,
        jnp.where(low == 0, packed[0], packed[1]),
        jnp.where(low == 2, packed[2], packed[3]),
    )
    plane = (code >> (3 * i)) % NZ
    return jnp.where(z < NZ // 2, plane, NZ - 1 - plane)


class Gather:
    def __init__(self, buf, rows, n, sems, place):
        cut = [rows // 16 * q // n * 16 for q in range(n + 1)]
        self.buf, self.n = buf, n
        self.chunks = [(a, b - a) for a, b in zip(cut, cut[1:])]
        self.zs, self.zr, self.gs, self.xs, self.xr, self.fs, self.fr = sems
        self.z, self.x, self.core = place
        self.gate = jnp.where(self.z < NZ // 2, NZ // 2, NZ // 2 - 1)

    def copy(self, plane, x, q, send, recv, z, to_x):
        start, size = self.chunks[q]
        ref = self.buf.at[plane, x, pl.ds(start, size)]
        return pltpu.make_async_remote_copy(
            src_ref=ref,
            dst_ref=ref,
            send_sem=send,
            recv_sem=recv,
            device_id={"ctx": z * 8 + to_x * 2 + self.core},
            device_id_type=MESH,
        )

    def along_z(self, plane, q, step):
        k = 0 if step > 0 else 1
        return self.copy(
            plane, self.x, q, self.zs.at[plane, q, k], self.zr.at[plane, q], self.z + step, self.x
        )

    def to_gate(self, q):
        return self.copy(
            self.z, self.x, q, self.gs.at[q], self.zr.at[self.z, q], self.gate, self.x
        )

    def goes(self, plane, step):
        if step > 0:
            return (plane <= self.z) & (self.z % (NZ // 2) < NZ // 2 - 1)
        return (plane >= self.z) & (self.z % (NZ // 2) > 0)

    def along_x(self, plane, q, k):
        to_x = (self.x + (1 if k == 0 else 3)) % NX
        return self.copy(
            plane, self.x, q, self.xs.at[plane, q, k], self.xr.at[plane, q, k], self.z, to_x
        )

    def came_x(self, plane, q, k):
        from_x = (self.x + (3 if k == 0 else 1)) % NX
        return self.copy(
            plane, from_x, q, self.xs.at[plane, q, k], self.xr.at[plane, q, k], self.z, from_x
        )

    def turn(self, q):
        return 0 if q < self.n // 2 else 1

    def onward(self, plane, q):
        k = self.turn(q)
        block_x = (self.x + (3 if k == 0 else 1)) % NX
        to_x = (self.x + (1 if k == 0 else 3)) % NX
        return self.copy(
            plane, block_x, q, self.fs.at[plane, q], self.fr.at[plane, q], self.z, to_x
        )

    def came_onward(self, plane, q):
        far_x = (self.x + 2) % NX
        return self.copy(
            plane, far_x, q, self.fs.at[plane, q], self.fr.at[plane, q], self.z, far_x
        )

    def source(self, q):
        self.to_gate(q).start()
        self.spread(self.z, q)

    def spread(self, plane, q):
        for step in (1, -1):

            @pl.when(self.goes(plane, step))
            def _():
                self.along_z(plane, q, step).start()

        self.along_x(plane, q, 0).start()
        self.along_x(plane, q, 1).start()

    def arrive(self, plane):
        for q in range(self.n):
            self.copy(
                plane, self.x, q, self.zs.at[plane, q, 0], self.zr.at[plane, q], self.z, self.x
            ).wait_recv()
            self.spread(plane, q)

    def pass_on(self, plane):
        for q in range(self.n):
            self.came_x(plane, q, self.turn(q)).wait_recv()
            self.onward(plane, q).start()

    def complete(self, plane):
        for q in range(self.n):
            self.came_x(plane, q, 1 - self.turn(q)).wait_recv()
        for q in range(self.n):
            self.came_onward(plane, q).wait_recv()

    def drain(self):
        for q in range(self.n):
            self.to_gate(q).wait_send()

        @pl.loop(0, NZ)
        def _(plane):
            for q in range(self.n):
                for step in (1, -1):

                    @pl.when(self.goes(plane, step))
                    def _():
                        self.along_z(plane, q, step).wait_send()

                self.along_x(plane, q, 0).wait_send()
                self.along_x(plane, q, 1).wait_send()
                self.onward(plane, q).wait_send()


def kernel(
    stored, owner_ref, doc_ref, starts_ref, freq_ref, wq, wk, wv, out,
    meta, table, wg, xa, acc, cosine, sine, select, unpack, pos_doc, q_doc,
    outgoing, middle, incoming, kv, qp, top, total, summed, scores,
    table_send, table_recv, own_sems, swap_send, swap_recv, act_send, act_recv,
    wzs, wzr, wgs, wxs, wxr, wfs, wfr,
    kzs, kzr, kgs, kxs, kxr, kfs, kfr,
    sib_send, sib_recv, q_send, q_recv,
):
    c = lax.axis_index("ctx")
    t = lax.axis_index("tp")
    z, x, core = c // 8, (c // 2) % NX, c % 2
    y, zh = t // 2, t % 2
    chip = c // 2
    cell = c % 8
    sib = chip * 2 + (1 - core)
    place = (z, x, core)
    first = core == 0
    weights = Gather(wg, WB, NQ, (wzs, wzr, wgs, wxs, wxr, wfs, wfr), place)
    keyvals = Gather(kv.at[core], KB, KQ, (kzs, kzr, kgs, kxs, kxr, kfs, kfr), place)

    def on_line(i):
        return ((z + i) % NZ) * 8 + cell

    def in_plane(i):
        return z * 8 + (cell + i) % 8

    def own_copies(w_third):
        refs = [wq.at[:, pl.ds(pl.multiple_of((core * 2 + g) * HEAD, HEAD), HEAD)] for g in range(2)]
        return [
            pltpu.make_async_copy(
                ref,
                wg.at[z, x, pl.ds(pl.multiple_of(core * 192 + g * 64, 64), 64)],
                own_sems.at[g],
            )
            for g, ref in enumerate(refs + [w_third])
        ]

    def swap_copies(w_third, mine):
        low = (1 - core) * 2
        refs = [wq.at[:, pl.ds(pl.multiple_of((low + g) * HEAD, HEAD), HEAD)] for g in range(2)]
        row = core if mine else 1 - core
        return [
            pltpu.make_async_remote_copy(
                src_ref=ref,
                dst_ref=wg.at[z, x, pl.ds(pl.multiple_of(row * 192 + g * 64, 64), 64)],
                send_sem=swap_send.at[g],
                recv_sem=swap_recv.at[g],
                device_id={"ctx": sib},
                device_id_type=MESH,
            )
            for g, ref in enumerate(refs + [w_third])
        ]

    own_acts_copy = pltpu.make_async_copy(stored, xa.at[t, core], own_sems.at[3])
    own_acts_copy.start()

    @pl.when(first)
    def _():
        for one in own_copies(wk):
            one.start()

    @pl.when(jnp.logical_not(first))
    def _():
        for one in own_copies(wv):
            one.start()

    meta[0:1, :] = owner_ref[...]
    meta[1:2, :] = doc_ref[...]

    barrier = pltpu.get_barrier_semaphore()

    @pl.loop(1, 8)
    def _(i):
        for to in (on_line(i), in_plane(i)):
            pl.semaphore_signal(barrier, inc=1, device_id={"ctx": to}, device_id_type=MESH)

    def y_peer(step):
        return ((y + step) % 4) * 2 + zh

    twin = y * 2 + (1 - zh)
    for to in (y_peer(1), y_peer(2), y_peer(3), twin):
        pl.semaphore_signal(barrier, inc=1, device_id={"tp": to}, device_id_type=MESH)
    pl.semaphore_wait(barrier, 7 + 7 + 4)

    @pl.when(first)
    def _():
        for one in swap_copies(wv, True):
            one.start()

    @pl.when(jnp.logical_not(first))
    def _():
        for one in swap_copies(wk, True):
            one.start()

    for one in own_copies(wk):
        one.wait()

    def source_half(which):
        for q in range(NQ // 2):
            weights.source(which * (NQ // 2) + q)

    @pl.when(first)
    def _():
        source_half(0)

    @pl.when(jnp.logical_not(first))
    def _():
        source_half(1)

    def act(src, slot, k, axis, to):
        return pltpu.make_async_remote_copy(
            src_ref=src,
            dst_ref=xa.at[slot, core],
            send_sem=act_send.at[k],
            recv_sem=act_recv.at[slot, core],
            device_id={axis: to},
            device_id_type=MESH,
        )

    def act_wait(slot, who):
        pltpu.make_async_remote_copy(
            src_ref=xa.at[slot, who],
            dst_ref=xa.at[slot, who],
            send_sem=act_send.at[0],
            recv_sem=act_recv.at[slot, who],
            device_id={"tp": t},
            device_id_type=MESH,
        ).wait_recv()

    own_acts = [act(stored, t, 0, "tp", twin)]
    own_acts += [act(stored, t, k, "tp", y_peer(k)) for k in (1, 3, 2)]
    own_acts += [act(stored, t, 4, "ctx", sib)]
    for one in own_acts:
        one.start()
    twin_acts = [act(xa.at[twin, core], twin, 4 + k, "tp", y_peer(k)) for k in (1, 3, 2)]
    twin_acts += [act(xa.at[twin, core], twin, 8, "ctx", sib)]
    across = [
        act(xa.at[y_peer(k), core], y_peer(k), 8 + k, "ctx", sib) for k in (1, 2, 3)
    ]
    across_twin = [
        act(xa.at[(y_peer(k) // 2) * 2 + (1 - zh), core], (y_peer(k) // 2) * 2 + (1 - zh), 11 + k, "ctx", sib)
        for k in (1, 2, 3)
    ]

    for one in swap_copies(wk, False):
        one.wait_recv()

    @pl.when(first)
    def _():
        source_half(1)

    @pl.when(jnp.logical_not(first))
    def _():
        source_half(0)

    def table_near(to):
        return pltpu.make_async_remote_copy(
            src_ref=meta,
            dst_ref=table.at[c],
            send_sem=table_send.at[0],
            recv_sem=table_recv.at[0],
            device_id={"ctx": to},
            device_id_type=MESH,
        )

    def table_far(to):
        ref = table.at[pl.ds(z * 8, 8)]
        return pltpu.make_async_remote_copy(
            src_ref=ref,
            dst_ref=ref,
            send_sem=table_send.at[1],
            recv_sem=table_recv.at[1],
            device_id={"ctx": to},
            device_id_type=MESH,
        )

    @pl.loop(1, 8)
    def _(i):
        table_near(in_plane(i)).start()

    pltpu.make_async_copy(meta, table.at[c], table_recv.at[0]).start()

    def table_onward():
        ref = table.at[pl.ds(z * 8, 8)]
        pltpu.make_async_copy(ref, ref, table_recv.at[0]).wait()

        @pl.loop(1, NZ)
        def _(i):
            table_far(on_line(i)).start()

    def plan():
        far = table.at[pl.ds(0, 56)]
        pltpu.make_async_copy(far, far, table_recv.at[1]).wait()
        owners = table[:, 0, :]
        docs = table[:, 1, :].astype(F32).astype(BF16)
        before_l = (iota((128, 128), 0) < iota((128, 128), 1)).astype(F32).astype(BF16)
        before_s = (iota((64, 64), 1) < iota((64, 64), 0)).astype(F32).astype(BF16)
        rows = iota((512, 128), 0)
        spread_rows = (iota((512, 64), 0) // 8 == iota((512, 64), 1)).astype(F32).astype(BF16)
        doc_tile = jnp.zeros((16, 128), F32)
        for oc in range(2):
            hit = owners == chip * 2 + oc
            hot = hit.astype(F32)
            hot16 = hot.astype(BF16)
            lane_before = dot(hot16, before_l)
            count = jnp.broadcast_to(jnp.sum(hot, axis=1, keepdims=True), (64, 128))
            before = jnp.broadcast_to(
                jnp.sum(dot(before_s, hot16), axis=1, keepdims=True), (64, 128)
            )
            rank1 = jnp.where(hit, before + lane_before + 1.0, 0.0)
            before_t = jnp.concatenate([before, before], axis=0).T[:, :64]
            count_t = jnp.concatenate([count, count], axis=0).T[:, :64]
            r64 = iota((128, 64), 0).astype(F32)
            shard_hot = jnp.where((before_t <= r64) & (r64 < before_t + count_t), 1.0, 0.0)
            shard_hot16 = shard_hot.astype(BF16)
            ranks = dot(shard_hot16, rank1.astype(BF16))
            found = ranks == iota((128, 128), 0).astype(F32) + 1.0
            lane = jnp.sum(
                jnp.where(found, iota((128, 128), 1).astype(F32), 0.0), axis=1, keepdims=True
            )
            doc = jnp.sum(
                jnp.where(found, dot(shard_hot16, docs), 0.0), axis=1, keepdims=True
            )
            shard = jnp.sum(
                shard_hot * iota((128, 64), 1).astype(F32), axis=1, keepdims=True
            )
            n_doc = starts_ref.shape[1]
            starts = jnp.broadcast_to(starts_ref[...].astype(F32), (128, n_doc))
            start = jnp.sum(
                jnp.where(doc == iota((128, n_doc), 1).astype(F32), starts, 0.0),
                axis=1,
                keepdims=True,
            )
            position = shard * 128.0 + lane - start
            angle = position * freq_ref[...]
            span = pl.ds(oc * 128, 128)
            cosine[span, :] = jnp.cos(angle)
            sign = jnp.where(iota((128, 128), 1) < 64, -1.0, 1.0)
            sine[span, :] = jnp.sin(angle) * sign
            doc_rows = jnp.broadcast_to(doc, (128, 128)).T
            doc_tile = jnp.where(iota((16, 128), 0) == oc, doc_rows[:16], doc_tile)
            begin = dot(spread_rows, before.astype(BF16))
            many = dot(spread_rows, count.astype(BF16))
            slot = (rows % CAP).astype(F32)
            chosen = (
                (iota((512, 128), 1).astype(F32) == begin + slot)
                & (slot < many)
                & ((rows // CAP) % 2 == oc)
            )
            select[:, oc * 128 : (oc + 1) * 128] = jnp.where(chosen, 1.0, 0.0).astype(BF16)
        pos_doc[...] = doc_tile.astype(BF16)
        mine = jnp.broadcast_to(owner_ref[...].astype(F32), (128, 128))
        mine_t = mine.T
        same = (mine == mine_t) & (iota((128, 128), 1) < iota((128, 128), 0))
        order = jnp.sum(jnp.where(same, 1.0, 0.0), axis=1, keepdims=True)
        col = iota((128, 512), 1)
        chip_col = (col // 16 % NZ) * NX + col // 128
        owner_col = (chip_col * 2 + (col // CAP) % 2).astype(F32)
        slot_col = (col % CAP).astype(F32)
        mine_col = jnp.broadcast_to(mine_t[:, :1], (128, 512))
        for hd in range(2):
            pick = (owner_col == mine_col) & (slot_col == order) & ((col // 8) % 2 == hd)
            unpack[hd] = jnp.where(pick, 1.0, 0.0).astype(BF16)
        q_doc[...] = jnp.broadcast_to(doc_ref[...].astype(F32), (128, 128)).T

    def project(plane):
        columns = []
        for xx in range(NX):
            for half_core in range(2):
                tiles = [
                    wg[plane, xx, half_core * 192 + g * 64 : half_core * 192 + (g + 1) * 64, :]
                    for g in range(3)
                ]
                columns.append(jnp.concatenate(tiles, axis=1))
        w = jnp.concatenate(columns, axis=0)
        acts = xa[plane].reshape(256, 512)
        acc[...] += dot(acts, w)

    acc[...] = jnp.zeros_like(acc)

    low = jnp.minimum(z, NZ - 1 - z)

    def when(row):
        return jnp.where(
            low < 2, jnp.where(low == 0, row[0], row[1]), jnp.where(low == 2, row[2], row[3])
        )

    def each(i, row, go):
        begin = when(row)

        @pl.when((i >= begin) & (i < begin + NZ))
        def _():
            go(plane_at(z, i - begin))

    def once(i, row, go):
        @pl.when(i == when(row))
        def _():
            go()

    def acts_near():
        for k in (1, 2, 3):
            act_wait(y_peer(k), core)
            across[k - 1].start()

    def acts_twin():
        act_wait(twin, core)
        for one in twin_acts:
            one.start()

    def acts_far():
        for k in (1, 2, 3):
            act_wait((y_peer(k) // 2) * 2 + (1 - zh), core)
            across_twin[k - 1].start()

    def all_acts():
        own_acts_copy.wait()

        @pl.loop(0, 8)
        def _(slot):
            act_wait(slot, 1 - core)

    def use_plane(plane):
        weights.complete(plane)
        project(plane)

    @pl.loop(0, NZ + max(WDONE))
    def _(i):
        @pl.when((i > 0) & (i < NZ))
        def _():
            weights.arrive(plane_at(z, i))

        once(i, (1, 1, 1, 1), table_onward)
        once(i, NEAR, acts_near)
        once(i, TWIN, acts_twin)
        once(i, PLAN, plan)
        once(i, FAR, acts_far)
        each(i, WPASS, weights.pass_on)
        once(i, WDONE, all_acts)
        each(i, WDONE, use_plane)

    def rotate(v):
        return v * cosine[...] + pltpu.roll(v, 64, 1) * sine[...]

    third = acc[:, 256:384]
    kv[core, z, x, 0:256, :] = jnp.where(first, rotate(third), third).astype(BF16)
    kv[core, z, x, 256:272, :] = pos_doc[...]
    for q in range(KQ):
        keyvals.source(q)
    blocks = []
    for hd in range(2):
        rotated = rotate(acc[:, hd * HEAD : (hd + 1) * HEAD]).astype(BF16)
        blocks.append(dot(select[...], rotated).reshape(64, 8, HEAD))
    outgoing[...] = jnp.concatenate(blocks, axis=1).astype(BF16)

    def q_far(i):
        return pltpu.make_async_remote_copy(
            src_ref=outgoing.at[pl.ds(((z + i) % NZ) * 8, 8)],
            dst_ref=middle.at[z],
            send_sem=q_send.at[0],
            recv_sem=q_recv.at[0],
            device_id={"ctx": on_line(i)},
            device_id_type=MESH,
        )

    def q_near(i):
        return pltpu.make_async_remote_copy(
            src_ref=middle.at[:, (cell + i) % 8],
            dst_ref=incoming.at[core, x],
            send_sem=q_send.at[1],
            recv_sem=q_recv.at[1],
            device_id={"ctx": in_plane(i)},
            device_id_type=MESH,
        )

    @pl.loop(1, NZ)
    def _(i):
        q_far(i).start()

    pltpu.make_async_copy(outgoing.at[pl.ds(z * 8, 8)], middle.at[z], q_recv.at[0]).start()

    def q_onward():
        pltpu.make_async_copy(middle, middle, q_recv.at[0]).wait()

        @pl.loop(1, 8)
        def _(i):
            q_near(i).start()

        pltpu.make_async_copy(middle.at[:, cell], incoming.at[core, x], q_recv.at[1]).start()

    def sibling(plane, who):
        return pltpu.make_async_remote_copy(
            src_ref=kv.at[who, plane],
            dst_ref=kv.at[who, plane],
            send_sem=sib_send.at[plane],
            recv_sem=sib_recv.at[plane],
            device_id={"ctx": sib},
            device_id_type=MESH,
        )

    top[...] = jnp.full_like(top, -1e30)
    total[...] = jnp.zeros_like(total)
    summed[...] = jnp.zeros_like(summed)
    factor2 = 1.4426950408889634 / HEAD**0.5

    def collect():
        pltpu.make_async_copy(incoming, incoming, q_recv.at[1]).wait()
        for who in range(2):
            block = incoming[who].reshape(512, HEAD)
            for hd in range(2):
                qp[who * 2 + hd] = dot(unpack[hd], block).astype(BF16)

    def masked_scores(plane, h0, key_doc):
        q = qp[h0 : h0 + 2].reshape(256, HEAD)
        query_doc = jnp.concatenate([q_doc[...]] * 2, axis=1)
        largest = None
        for xx in range(NX):
            block = lax.dot_general(
                q,
                kv[0, plane, xx, 0:256, :],
                (((1,), (1,)), ((), ())),
                preferred_element_type=F32,
            )
            kept = query_doc == key_doc[xx]
            block = jnp.where(jnp.concatenate([kept] * 2, axis=0), block * factor2, -2e30)
            scores[h0 * HEAD : h0 * HEAD + 256, xx * 256 : (xx + 1) * 256] = block
            here = jnp.maximum(block[:, :HEAD], block[:, HEAD:])
            largest = here if largest is None else jnp.maximum(largest, here)
        return largest

    def weigh(plane, h0, largest):
        two = slice(h0, h0 + 2)
        old = top[two].reshape(256, HEAD)
        new = jnp.maximum(old, jnp.max(largest, axis=1, keepdims=True))
        fall = jnp.exp2(old - new)
        lanes = total[two].reshape(256, HEAD) * fall
        mixed = summed[two].reshape(256, HEAD) * fall
        wide = jnp.concatenate([new, new], axis=1)
        for xx in range(NX):
            block = scores[h0 * HEAD : h0 * HEAD + 256, xx * 256 : (xx + 1) * 256]
            block = jnp.exp2(block - wide)
            lanes = lanes + (block[:, :HEAD] + block[:, HEAD:])
            mixed = mixed + dot(block.astype(BF16), kv[1, plane, xx, 0:256, :])
        total[two] = lanes.reshape(2, 128, HEAD)
        summed[two] = mixed.reshape(2, 128, HEAD)
        top[two] = new.reshape(2, 128, HEAD)

    def attend(plane):
        key_doc = []
        for xx in range(NX):
            tile = kv[0, plane, xx, 256:272, :].astype(F32)
            key_doc.append(jnp.concatenate([tile[0:1, :], tile[1:2, :]], axis=1))
        one = masked_scores(plane, 0, key_doc)
        two = masked_scores(plane, 2, key_doc)
        weigh(plane, 0, one)
        weigh(plane, 2, two)

    def finish_plane(plane):
        keyvals.complete(plane)
        sibling(plane, core).start()

    def attend_plane(plane):
        sibling(plane, 1 - core).wait_recv()
        attend(plane)

    @pl.loop(0, NZ + max(ATT))
    def _(i):
        @pl.when((i > 0) & (i < NZ))
        def _():
            keyvals.arrive(plane_at(z, i))

        each(i, KPASS, keyvals.pass_on)
        once(i, QMID, q_onward)
        each(i, KDONE, finish_plane)
        once(i, QGOT, collect)
        each(i, ATT, attend_plane)

    for h in range(4):
        whole = jnp.sum(total[h], axis=1, keepdims=True)
        out[:, h * HEAD : (h + 1) * HEAD] = (summed[h] / whole).astype(BF16)

    for one in swap_copies(wk, True):
        one.wait_send()
    for one in own_acts + twin_acts + across + across_twin:
        one.wait_send()
    weights.drain()
    keyvals.drain()

    @pl.loop(0, NZ)
    def _(plane):
        sibling(plane, core).wait_send()

    near = table.at[pl.ds(0, 7)]
    pltpu.make_async_copy(near, near, table_send.at[0]).wait()
    far = table.at[pl.ds(0, 56)]
    pltpu.make_async_copy(far, far, table_send.at[1]).wait()
    for k in range(2):
        pltpu.make_async_copy(
            middle.at[pl.ds(0, 7)], middle.at[pl.ds(0, 7)], q_send.at[k]
        ).wait()


def body(stored, source_owner, doc_ids, doc_starts, wq, wk, wv):
    half = HEAD // 2
    freqs = np.float32(ROPE_BASE) ** (-np.arange(half, dtype=np.float32) * np.float32(2.0 / HEAD))
    freqs = jnp.asarray(np.concatenate([freqs, freqs])[None, :], F32)
    dma = pltpu.SemaphoreType.DMA

    def ring_sems(n):
        shapes = ((NZ, n, 2), (NZ, n), (n,), (NZ, n, 2), (NZ, n, 2), (NZ, n), (NZ, n))
        return [dma(shape) for shape in shapes]

    scratch = [
        pltpu.VMEM((2, 128), jnp.int32),
        pltpu.VMEM((NCTX, 2, 128), jnp.int32),
        pltpu.VMEM((NZ, NX, WB, HEAD), BF16),
        pltpu.VMEM((8, 2, 128, 512), BF16),
        pltpu.VMEM((256, 384), F32),
        pltpu.VMEM((256, HEAD), F32),
        pltpu.VMEM((256, HEAD), F32),
        pltpu.VMEM((512, 256), BF16),
        pltpu.VMEM((2, 128, 512), BF16),
        pltpu.VMEM((16, 128), BF16),
        pltpu.VMEM((128, 128), F32),
        pltpu.VMEM((NCTX, 16, HEAD), BF16),
        pltpu.VMEM((NZ, 8, 16, HEAD), BF16),
        pltpu.VMEM((2, NX, NZ, 16, HEAD), BF16),
        pltpu.VMEM((2, NZ, NX, KB, HEAD), BF16),
        pltpu.VMEM((4, 128, HEAD), BF16),
        pltpu.VMEM((4, 128, HEAD), F32),
        pltpu.VMEM((4, 128, HEAD), F32),
        pltpu.VMEM((4, 128, HEAD), F32),
        pltpu.VMEM((512, 1024), F32),
        dma((2,)), dma((2,)), dma((4,)), dma((3,)), dma((3,)), dma((15,)), dma((8, 2)),
        *ring_sems(NQ),
        *ring_sems(KQ),
        dma((NZ,)), dma((NZ,)), dma((2,)), dma((2,)),
    ]
    vmem = pl.BlockSpec(memory_space=pltpu.VMEM)
    hbm = pl.BlockSpec(memory_space=pltpu.HBM)
    return pl.pallas_call(
        kernel,
        out_shape=jax.ShapeDtypeStruct((128, 512), BF16),
        in_specs=[hbm] + [vmem] * 4 + [hbm] * 3,
        out_specs=vmem,
        scratch_shapes=scratch,
        compiler_params=pltpu.CompilerParams(
            collective_id=0, has_side_effects=True, vmem_limit_bytes=62 << 20
        ),
        name="layer",
    )(stored, source_owner[None, :], doc_ids[None, :], doc_starts[None, :], freqs, wq, wk, wv)


def solution(mesh):
    return jax.shard_map(
        body,
        mesh=mesh,
        in_specs=(
            P("ctx", "tp"), P("ctx"), P("ctx"), P(), P("ctx", "tp"), P("ctx", "tp"), P("ctx", "tp"),
        ),
        out_specs=P("ctx", "tp"),
        check_vma=False,
    )
```

```python
import functools

import jax
import jax.numpy as jnp
import numpy as np
from jax import lax
from jax.experimental import pallas as pl
from jax.experimental.pallas import tpu as pltpu
from jax.sharding import PartitionSpec as P

HEAD = 128
ROPE_BASE = 500000.0
MESH = pl.DeviceIdType.MESH
F32 = jnp.float32
BF16 = jnp.bfloat16
NZ, NX = 8, 4
NCTX = 64
CAP = 4
WB = 384
KB = 272
NQ = 2
KQ = 2
NEAR = (1, 2, 3, 5)
PLAN = (4, 5, 7, 8)
TWIN = (4, 5, 7, 8)
FAR = (6, 7, 8, 9)
WPASS = (1, 2, 4, 6)
WDONE = (8, 8, 9, 10)
KPASS = (1, 2, 4, 6)
KDONE = (3, 5, 7, 9)
QMID = (3, 4, 7, 8)
QGOT = (5, 6, 9, 10)
ATT = (5, 6, 9, 10)
ORDER = (
    (0, 1, 2, 3, 4, 5, 6, 7),
    (1, 0, 2, 3, 4, 5, 6, 7),
    (2, 3, 1, 4, 0, 5, 6, 7),
    (3, 4, 2, 5, 1, 6, 7, 0),
)


def dot(a, b):
    return jnp.dot(a, b, preferred_element_type=F32)


def iota(shape, dim):
    return lax.broadcasted_iota(jnp.int32, shape, dim)


def plane_at(z, i):
    low = jnp.minimum(z, NZ - 1 - z)
    packed = [sum(p << (3 * n) for n, p in enumerate(row)) for row in ORDER]
    code = jnp.where(
        low < 2,
        jnp.where(low == 0, packed[0], packed[1]),
        jnp.where(low == 2, packed[2], packed[3]),
    )
    plane = (code >> (3 * i)) % NZ
    return jnp.where(z < NZ // 2, plane, NZ - 1 - plane)


class Gather:
    def __init__(self, buf, rows, n, sems, place):
        cut = [rows // 16 * q // n * 16 for q in range(n + 1)]
        self.buf, self.n = buf, n
        self.chunks = [(a, b - a) for a, b in zip(cut, cut[1:])]
        self.zs, self.zr, self.gs, self.xs, self.xr, self.fs, self.fr = sems
        self.z, self.x, self.core = place
        self.gate = jnp.where(self.z < NZ // 2, NZ // 2, NZ // 2 - 1)

    def copy(self, plane, x, q, send, recv, z, to_x):
        start, size = self.chunks[q]
        ref = self.buf.at[plane, x, pl.ds(start, size)]
        return pltpu.make_async_remote_copy(
            src_ref=ref,
            dst_ref=ref,
            send_sem=send,
            recv_sem=recv,
            device_id={"ctx": z * 8 + to_x * 2 + self.core},
            device_id_type=MESH,
        )

    def along_z(self, plane, q, step):
        k = 0 if step > 0 else 1
        return self.copy(
            plane, self.x, q, self.zs.at[plane, q, k], self.zr.at[plane, q], self.z + step, self.x
        )

    def to_gate(self, q):
        return self.copy(
            self.z, self.x, q, self.gs.at[q], self.zr.at[self.z, q], self.gate, self.x
        )

    def goes(self, plane, step):
        if step > 0:
            return (plane <= self.z) & (self.z % (NZ // 2) < NZ // 2 - 1)
        return (plane >= self.z) & (self.z % (NZ // 2) > 0)

    def along_x(self, plane, q, k):
        to_x = (self.x + (1 if k == 0 else 3)) % NX
        return self.copy(
            plane, self.x, q, self.xs.at[plane, q, k], self.xr.at[plane, q, k], self.z, to_x
        )

    def came_x(self, plane, q, k):
        from_x = (self.x + (3 if k == 0 else 1)) % NX
        return self.copy(
            plane, from_x, q, self.xs.at[plane, q, k], self.xr.at[plane, q, k], self.z, from_x
        )

    def turn(self, q):
        return 0 if q < self.n // 2 else 1

    def onward(self, plane, q):
        k = self.turn(q)
        block_x = (self.x + (3 if k == 0 else 1)) % NX
        to_x = (self.x + (1 if k == 0 else 3)) % NX
        return self.copy(
            plane, block_x, q, self.fs.at[plane, q], self.fr.at[plane, q], self.z, to_x
        )

    def came_onward(self, plane, q):
        far_x = (self.x + 2) % NX
        return self.copy(
            plane, far_x, q, self.fs.at[plane, q], self.fr.at[plane, q], self.z, far_x
        )

    def source(self, q):
        self.to_gate(q).start()
        self.spread(self.z, q)

    def spread(self, plane, q):
        for step in (1, -1):

            @pl.when(self.goes(plane, step))
            def _():
                self.along_z(plane, q, step).start()

        self.along_x(plane, q, 0).start()
        self.along_x(plane, q, 1).start()

    def arrive(self, plane):
        for q in range(self.n):
            self.copy(
                plane, self.x, q, self.zs.at[plane, q, 0], self.zr.at[plane, q], self.z, self.x
            ).wait_recv()
            self.spread(plane, q)

    def pass_on(self, plane):
        for q in range(self.n):
            self.came_x(plane, q, self.turn(q)).wait_recv()
            self.onward(plane, q).start()

    def complete(self, plane):
        for q in range(self.n):
            self.came_x(plane, q, 1 - self.turn(q)).wait_recv()
        for q in range(self.n):
            self.came_onward(plane, q).wait_recv()

    def drain(self):
        for q in range(self.n):
            self.to_gate(q).wait_send()

        @pl.loop(0, NZ)
        def _(plane):
            for q in range(self.n):
                for step in (1, -1):

                    @pl.when(self.goes(plane, step))
                    def _():
                        self.along_z(plane, q, step).wait_send()

                self.along_x(plane, q, 0).wait_send()
                self.along_x(plane, q, 1).wait_send()
                self.onward(plane, q).wait_send()


def kernel(
    stored, owner_ref, doc_ref, starts_ref, freq_ref, wq, wk, wv, out,
    meta, table, wg, xa, acc, cosine, sine, select, unpack, pos_doc, q_doc,
    outgoing, middle, incoming, kv, qp, top, total, summed, scores,
    table_send, table_recv, own_sems, swap_send, swap_recv, act_send, act_recv,
    wzs, wzr, wgs, wxs, wxr, wfs, wfr,
    kzs, kzr, kgs, kxs, kxr, kfs, kfr,
    sib_send, sib_recv, q_send, q_recv,
):
    c = lax.axis_index("ctx")
    t = lax.axis_index("tp")
    z, x, core = c // 8, (c // 2) % NX, c % 2
    y, zh = t // 2, t % 2
    chip = c // 2
    cell = c % 8
    sib = chip * 2 + (1 - core)
    place = (z, x, core)
    first = core == 0
    weights = Gather(wg, WB, NQ, (wzs, wzr, wgs, wxs, wxr, wfs, wfr), place)
    keyvals = Gather(kv.at[core], KB, KQ, (kzs, kzr, kgs, kxs, kxr, kfs, kfr), place)

    def on_line(i):
        return ((z + i) % NZ) * 8 + cell

    def in_plane(i):
        return z * 8 + (cell + i) % 8

    def own_copies(w_third):
        refs = [wq.at[:, pl.ds(pl.multiple_of((core * 2 + g) * HEAD, HEAD), HEAD)] for g in range(2)]
        return [
            pltpu.make_async_copy(
                ref,
                wg.at[z, x, pl.ds(pl.multiple_of(core * 192 + g * 64, 64), 64)],
                own_sems.at[g],
            )
            for g, ref in enumerate(refs + [w_third])
        ]

    def swap_copies(w_third, mine):
        low = (1 - core) * 2
        refs = [wq.at[:, pl.ds(pl.multiple_of((low + g) * HEAD, HEAD), HEAD)] for g in range(2)]
        row = core if mine else 1 - core
        return [
            pltpu.make_async_remote_copy(
                src_ref=ref,
                dst_ref=wg.at[z, x, pl.ds(pl.multiple_of(row * 192 + g * 64, 64), 64)],
                send_sem=swap_send.at[g],
                recv_sem=swap_recv.at[g],
                device_id={"ctx": sib},
                device_id_type=MESH,
            )
            for g, ref in enumerate(refs + [w_third])
        ]

    own_acts_copy = pltpu.make_async_copy(stored, xa.at[t, core], own_sems.at[3])
    own_acts_copy.start()

    @pl.when(first)
    def _():
        for one in own_copies(wk):
            one.start()

    @pl.when(jnp.logical_not(first))
    def _():
        for one in own_copies(wv):
            one.start()

    meta[0:1, :] = owner_ref[...]
    meta[1:2, :] = doc_ref[...]

    barrier = pltpu.get_barrier_semaphore()

    @pl.loop(1, 8)
    def _(i):
        for to in (on_line(i), in_plane(i)):
            pl.semaphore_signal(barrier, inc=1, device_id={"ctx": to}, device_id_type=MESH)

    def y_peer(step):
        return ((y + step) % 4) * 2 + zh

    twin = y * 2 + (1 - zh)
    for to in (y_peer(1), y_peer(2), y_peer(3), twin):
        pl.semaphore_signal(barrier, inc=1, device_id={"tp": to}, device_id_type=MESH)
    pl.semaphore_wait(barrier, 7 + 7 + 4)

    @pl.when(first)
    def _():
        for one in swap_copies(wv, True):
            one.start()

    @pl.when(jnp.logical_not(first))
    def _():
        for one in swap_copies(wk, True):
            one.start()

    for one in own_copies(wk):
        one.wait()

    def source_half(which):
        for q in range(NQ // 2):
            weights.source(which * (NQ // 2) + q)

    @pl.when(first)
    def _():
        source_half(0)

    @pl.when(jnp.logical_not(first))
    def _():
        source_half(1)

    def act(src, slot, k, axis, to):
        return pltpu.make_async_remote_copy(
            src_ref=src,
            dst_ref=xa.at[slot, core],
            send_sem=act_send.at[k],
            recv_sem=act_recv.at[slot, core],
            device_id={axis: to},
            device_id_type=MESH,
        )

    def act_wait(slot, who):
        pltpu.make_async_remote_copy(
            src_ref=xa.at[slot, who],
            dst_ref=xa.at[slot, who],
            send_sem=act_send.at[0],
            recv_sem=act_recv.at[slot, who],
            device_id={"tp": t},
            device_id_type=MESH,
        ).wait_recv()

    own_acts = [act(stored, t, 0, "tp", twin)]
    own_acts += [act(stored, t, k, "tp", y_peer(k)) for k in (1, 3, 2)]
    own_acts += [act(stored, t, 4, "ctx", sib)]
    for one in own_acts:
        one.start()
    twin_acts = [act(xa.at[twin, core], twin, 4 + k, "tp", y_peer(k)) for k in (1, 3, 2)]
    twin_acts += [act(xa.at[twin, core], twin, 8, "ctx", sib)]
    across = [
        act(xa.at[y_peer(k), core], y_peer(k), 8 + k, "ctx", sib) for k in (1, 2, 3)
    ]
    across_twin = [
        act(xa.at[(y_peer(k) // 2) * 2 + (1 - zh), core], (y_peer(k) // 2) * 2 + (1 - zh), 11 + k, "ctx", sib)
        for k in (1, 2, 3)
    ]

    for one in swap_copies(wk, False):
        one.wait_recv()

    @pl.when(first)
    def _():
        source_half(1)

    @pl.when(jnp.logical_not(first))
    def _():
        source_half(0)

    def table_near(to):
        return pltpu.make_async_remote_copy(
            src_ref=meta,
            dst_ref=table.at[c],
            send_sem=table_send.at[0],
            recv_sem=table_recv.at[0],
            device_id={"ctx": to},
            device_id_type=MESH,
        )

    def table_far(to):
        ref = table.at[pl.ds(z * 8, 8)]
        return pltpu.make_async_remote_copy(
            src_ref=ref,
            dst_ref=ref,
            send_sem=table_send.at[1],
            recv_sem=table_recv.at[1],
            device_id={"ctx": to},
            device_id_type=MESH,
        )

    @pl.loop(1, 8)
    def _(i):
        table_near(in_plane(i)).start()

    pltpu.make_async_copy(meta, table.at[c], table_recv.at[0]).start()

    def table_onward():
        ref = table.at[pl.ds(z * 8, 8)]
        pltpu.make_async_copy(ref, ref, table_recv.at[0]).wait()

        @pl.loop(1, NZ)
        def _(i):
            table_far(on_line(i)).start()

    def plan():
        far = table.at[pl.ds(0, 56)]
        pltpu.make_async_copy(far, far, table_recv.at[1]).wait()
        owners = table[:, 0, :]
        docs = table[:, 1, :].astype(F32).astype(BF16)
        before_l = (iota((128, 128), 0) < iota((128, 128), 1)).astype(F32).astype(BF16)
        before_s = (iota((64, 64), 1) < iota((64, 64), 0)).astype(F32).astype(BF16)
        rows = iota((512, 128), 0)
        spread_rows = (iota((512, 64), 0) // 8 == iota((512, 64), 1)).astype(F32).astype(BF16)
        doc_tile = jnp.zeros((16, 128), F32)
        for oc in range(2):
            hit = owners == chip * 2 + oc
            hot = hit.astype(F32)
            hot16 = hot.astype(BF16)
            lane_before = dot(hot16, before_l)
            count = jnp.broadcast_to(jnp.sum(hot, axis=1, keepdims=True), (64, 128))
            before = jnp.broadcast_to(
                jnp.sum(dot(before_s, hot16), axis=1, keepdims=True), (64, 128)
            )
            rank1 = jnp.where(hit, before + lane_before + 1.0, 0.0)
            before_t = jnp.concatenate([before, before], axis=0).T[:, :64]
            count_t = jnp.concatenate([count, count], axis=0).T[:, :64]
            r64 = iota((128, 64), 0).astype(F32)
            shard_hot = jnp.where((before_t <= r64) & (r64 < before_t + count_t), 1.0, 0.0)
            shard_hot16 = shard_hot.astype(BF16)
            ranks = dot(shard_hot16, rank1.astype(BF16))
            found = ranks == iota((128, 128), 0).astype(F32) + 1.0
            lane = jnp.sum(
                jnp.where(found, iota((128, 128), 1).astype(F32), 0.0), axis=1, keepdims=True
            )
            doc = jnp.sum(
                jnp.where(found, dot(shard_hot16, docs), 0.0), axis=1, keepdims=True
            )
            shard = jnp.sum(
                shard_hot * iota((128, 64), 1).astype(F32), axis=1, keepdims=True
            )
            n_doc = starts_ref.shape[1]
            starts = jnp.broadcast_to(starts_ref[...].astype(F32), (128, n_doc))
            start = jnp.sum(
                jnp.where(doc == iota((128, n_doc), 1).astype(F32), starts, 0.0),
                axis=1,
                keepdims=True,
            )
            position = shard * 128.0 + lane - start
            angle = position * freq_ref[...]
            span = pl.ds(oc * 128, 128)
            cosine[span, :] = jnp.cos(angle)
            sign = jnp.where(iota((128, 128), 1) < 64, -1.0, 1.0)
            sine[span, :] = jnp.sin(angle) * sign
            doc_rows = jnp.broadcast_to(doc, (128, 128)).T
            doc_tile = jnp.where(iota((16, 128), 0) == oc, doc_rows[:16], doc_tile)
            begin = dot(spread_rows, before.astype(BF16))
            many = dot(spread_rows, count.astype(BF16))
            slot = (rows % CAP).astype(F32)
            chosen = (
                (iota((512, 128), 1).astype(F32) == begin + slot)
                & (slot < many)
                & ((rows // CAP) % 2 == oc)
            )
            select[:, oc * 128 : (oc + 1) * 128] = jnp.where(chosen, 1.0, 0.0).astype(BF16)
        pos_doc[...] = doc_tile.astype(BF16)
        mine = jnp.broadcast_to(owner_ref[...].astype(F32), (128, 128))
        mine_t = mine.T
        same = (mine == mine_t) & (iota((128, 128), 1) < iota((128, 128), 0))
        order = jnp.sum(jnp.where(same, 1.0, 0.0), axis=1, keepdims=True)
        col = iota((128, 512), 1)
        chip_col = (col // 16 % NZ) * NX + col // 128
        owner_col = (chip_col * 2 + (col // CAP) % 2).astype(F32)
        slot_col = (col % CAP).astype(F32)
        mine_col = jnp.broadcast_to(mine_t[:, :1], (128, 512))
        for hd in range(2):
            pick = (owner_col == mine_col) & (slot_col == order) & ((col // 8) % 2 == hd)
            unpack[hd] = jnp.where(pick, 1.0, 0.0).astype(BF16)
        q_doc[...] = jnp.broadcast_to(doc_ref[...].astype(F32), (128, 128)).T

    def project(plane):
        columns = []
        for xx in range(NX):
            for half_core in range(2):
                tiles = [
                    wg[plane, xx, half_core * 192 + g * 64 : half_core * 192 + (g + 1) * 64, :]
                    for g in range(3)
                ]
                columns.append(jnp.concatenate(tiles, axis=1))
        w = jnp.concatenate(columns, axis=0)
        acts = xa[plane].reshape(256, 512)
        acc[...] += dot(acts, w)

    acc[...] = jnp.zeros_like(acc)

    low = jnp.minimum(z, NZ - 1 - z)

    def when(row):
        return jnp.where(
            low < 2, jnp.where(low == 0, row[0], row[1]), jnp.where(low == 2, row[2], row[3])
        )

    def each(i, row, go):
        begin = when(row)

        @pl.when((i >= begin) & (i < begin + NZ))
        def _():
            go(plane_at(z, i - begin))

    def once(i, row, go):
        @pl.when(i == when(row))
        def _():
            go()

    def acts_near():
        for k in (1, 2, 3):
            act_wait(y_peer(k), core)
            across[k - 1].start()

    def acts_twin():
        act_wait(twin, core)
        for one in twin_acts:
            one.start()

    def acts_far():
        for k in (1, 2, 3):
            act_wait((y_peer(k) // 2) * 2 + (1 - zh), core)
            across_twin[k - 1].start()

    def all_acts():
        own_acts_copy.wait()

        @pl.loop(0, 8)
        def _(slot):
            act_wait(slot, 1 - core)

    def use_plane(plane):
        weights.complete(plane)
        project(plane)

    @pl.loop(0, NZ + max(WDONE))
    def _(i):
        @pl.when((i > 0) & (i < NZ))
        def _():
            weights.arrive(plane_at(z, i))

        once(i, (1, 1, 1, 1), table_onward)
        once(i, NEAR, acts_near)
        once(i, TWIN, acts_twin)
        once(i, PLAN, plan)
        once(i, FAR, acts_far)
        each(i, WPASS, weights.pass_on)
        once(i, WDONE, all_acts)
        each(i, WDONE, use_plane)

    def rotate(v):
        return v * cosine[...] + pltpu.roll(v, 64, 1) * sine[...]

    third = acc[:, 256:384]
    kv[core, z, x, 0:256, :] = jnp.where(first, rotate(third), third).astype(BF16)
    kv[core, z, x, 256:272, :] = pos_doc[...]
    for q in range(KQ):
        keyvals.source(q)
    blocks = []
    for hd in range(2):
        rotated = rotate(acc[:, hd * HEAD : (hd + 1) * HEAD]).astype(BF16)
        blocks.append(dot(select[...], rotated).reshape(64, 8, HEAD))
    outgoing[...] = jnp.concatenate(blocks, axis=1).astype(BF16)

    def q_far(i):
        return pltpu.make_async_remote_copy(
            src_ref=outgoing.at[pl.ds(((z + i) % NZ) * 8, 8)],
            dst_ref=middle.at[z],
            send_sem=q_send.at[0],
            recv_sem=q_recv.at[0],
            device_id={"ctx": on_line(i)},
            device_id_type=MESH,
        )

    def q_near(i):
        return pltpu.make_async_remote_copy(
            src_ref=middle.at[:, (cell + i) % 8],
            dst_ref=incoming.at[core, x],
            send_sem=q_send.at[1],
            recv_sem=q_recv.at[1],
            device_id={"ctx": in_plane(i)},
            device_id_type=MESH,
        )

    @pl.loop(1, NZ)
    def _(i):
        q_far(i).start()

    pltpu.make_async_copy(outgoing.at[pl.ds(z * 8, 8)], middle.at[z], q_recv.at[0]).start()

    def q_onward():
        pltpu.make_async_copy(middle, middle, q_recv.at[0]).wait()

        @pl.loop(1, 8)
        def _(i):
            q_near(i).start()

        pltpu.make_async_copy(middle.at[:, cell], incoming.at[core, x], q_recv.at[1]).start()

    def sibling(plane, who):
        return pltpu.make_async_remote_copy(
            src_ref=kv.at[who, plane],
            dst_ref=kv.at[who, plane],
            send_sem=sib_send.at[plane],
            recv_sem=sib_recv.at[plane],
            device_id={"ctx": sib},
            device_id_type=MESH,
        )

    top[...] = jnp.full_like(top, -1e30)
    total[...] = jnp.zeros_like(total)
    summed[...] = jnp.zeros_like(summed)
    factor2 = 1.4426950408889634 / HEAD**0.5

    def collect():
        pltpu.make_async_copy(incoming, incoming, q_recv.at[1]).wait()
        for who in range(2):
            block = incoming[who].reshape(512, HEAD)
            for hd in range(2):
                qp[who * 2 + hd] = dot(unpack[hd], block).astype(BF16)

    def masked_scores(plane, h0, key_doc):
        q = qp[h0 : h0 + 2].reshape(256, HEAD)
        query_doc = jnp.concatenate([q_doc[...]] * 2, axis=1)
        largest = None
        for xx in range(NX):
            block = lax.dot_general(
                q,
                kv[0, plane, xx, 0:256, :],
                (((1,), (1,)), ((), ())),
                preferred_element_type=F32,
            )
            kept = query_doc == key_doc[xx]
            block = jnp.where(jnp.concatenate([kept] * 2, axis=0), block * factor2, -2e30)
            scores[h0 * HEAD : h0 * HEAD + 256, xx * 256 : (xx + 1) * 256] = block
            here = jnp.maximum(block[:, :HEAD], block[:, HEAD:])
            largest = here if largest is None else jnp.maximum(largest, here)
        return largest

    def weigh(plane, h0, largest):
        two = slice(h0, h0 + 2)
        old = top[two].reshape(256, HEAD)
        new = jnp.maximum(old, jnp.max(largest, axis=1, keepdims=True))
        fall = jnp.exp2(old - new)
        lanes = total[two].reshape(256, HEAD) * fall
        mixed = summed[two].reshape(256, HEAD) * fall
        wide = jnp.concatenate([new, new], axis=1)
        for xx in range(NX):
            block = scores[h0 * HEAD : h0 * HEAD + 256, xx * 256 : (xx + 1) * 256]
            block = jnp.exp2(block - wide)
            lanes = lanes + (block[:, :HEAD] + block[:, HEAD:])
            mixed = mixed + dot(block.astype(BF16), kv[1, plane, xx, 0:256, :])
        total[two] = lanes.reshape(2, 128, HEAD)
        summed[two] = mixed.reshape(2, 128, HEAD)
        top[two] = new.reshape(2, 128, HEAD)

    def attend(plane):
        key_doc = []
        for xx in range(NX):
            tile = kv[0, plane, xx, 256:272, :].astype(F32)
            key_doc.append(jnp.concatenate([tile[0:1, :], tile[1:2, :]], axis=1))
        one = masked_scores(plane, 0, key_doc)
        two = masked_scores(plane, 2, key_doc)
        weigh(plane, 0, one)
        weigh(plane, 2, two)

    def finish_plane(plane):
        keyvals.complete(plane)
        sibling(plane, core).start()

    def attend_plane(plane):
        sibling(plane, 1 - core).wait_recv()
        attend(plane)

    @pl.loop(0, NZ + max(ATT))
    def _(i):
        @pl.when((i > 0) & (i < NZ))
        def _():
            keyvals.arrive(plane_at(z, i))

        each(i, KPASS, keyvals.pass_on)
        once(i, QMID, q_onward)
        each(i, KDONE, finish_plane)
        once(i, QGOT, collect)
        each(i, ATT, attend_plane)

    for h in range(4):
        whole = jnp.sum(total[h], axis=1, keepdims=True)
        out[:, h * HEAD : (h + 1) * HEAD] = (summed[h] / whole).astype(BF16)

    for one in swap_copies(wk, True):
        one.wait_send()
    for one in own_acts + twin_acts + across + across_twin:
        one.wait_send()
    weights.drain()
    keyvals.drain()

    @pl.loop(0, NZ)
    def _(plane):
        sibling(plane, core).wait_send()

    near = table.at[pl.ds(0, 7)]
    pltpu.make_async_copy(near, near, table_send.at[0]).wait()
    far = table.at[pl.ds(0, 56)]
    pltpu.make_async_copy(far, far, table_send.at[1]).wait()
    for k in range(2):
        pltpu.make_async_copy(
            middle.at[pl.ds(0, 7)], middle.at[pl.ds(0, 7)], q_send.at[k]
        ).wait()


def body(stored, source_owner, doc_ids, doc_starts, wq, wk, wv):
    half = HEAD // 2
    freqs = np.float32(ROPE_BASE) ** (-np.arange(half, dtype=np.float32) * np.float32(2.0 / HEAD))
    freqs = jnp.asarray(np.concatenate([freqs, freqs])[None, :], F32)
    dma = pltpu.SemaphoreType.DMA

    def ring_sems(n):
        shapes = ((NZ, n, 2), (NZ, n), (n,), (NZ, n, 2), (NZ, n, 2), (NZ, n), (NZ, n))
        return [dma(shape) for shape in shapes]

    scratch = [
        pltpu.VMEM((2, 128), jnp.int32),
        pltpu.VMEM((NCTX, 2, 128), jnp.int32),
        pltpu.VMEM((NZ, NX, WB, HEAD), BF16),
        pltpu.VMEM((8, 2, 128, 512), BF16),
        pltpu.VMEM((256, 384), F32),
        pltpu.VMEM((256, HEAD), F32),
        pltpu.VMEM((256, HEAD), F32),
        pltpu.VMEM((512, 256), BF16),
        pltpu.VMEM((2, 128, 512), BF16),
        pltpu.VMEM((16, 128), BF16),
        pltpu.VMEM((128, 128), F32),
        pltpu.VMEM((NCTX, 16, HEAD), BF16),
        pltpu.VMEM((NZ, 8, 16, HEAD), BF16),
        pltpu.VMEM((2, NX, NZ, 16, HEAD), BF16),
        pltpu.VMEM((2, NZ, NX, KB, HEAD), BF16),
        pltpu.VMEM((4, 128, HEAD), BF16),
        pltpu.VMEM((4, 128, HEAD), F32),
        pltpu.VMEM((4, 128, HEAD), F32),
        pltpu.VMEM((4, 128, HEAD), F32),
        pltpu.VMEM((512, 1024), F32),
        dma((2,)), dma((2,)), dma((4,)), dma((3,)), dma((3,)), dma((15,)), dma((8, 2)),
        *ring_sems(NQ),
        *ring_sems(KQ),
        dma((NZ,)), dma((NZ,)), dma((2,)), dma((2,)),
    ]
    vmem = pl.BlockSpec(memory_space=pltpu.VMEM)
    hbm = pl.BlockSpec(memory_space=pltpu.HBM)
    return pl.pallas_call(
        kernel,
        out_shape=jax.ShapeDtypeStruct((128, 512), BF16),
        in_specs=[hbm] + [vmem] * 4 + [hbm] * 3,
        out_specs=vmem,
        scratch_shapes=scratch,
        compiler_params=pltpu.CompilerParams(
            collective_id=0, has_side_effects=True, vmem_limit_bytes=62 << 20
        ),
        name="layer",
    )(stored, source_owner[None, :], doc_ids[None, :], doc_starts[None, :], freqs, wq, wk, wv)


def solution(mesh):
    return jax.shard_map(
        body,
        mesh=mesh,
        in_specs=(
            P("ctx", "tp"), P("ctx"), P("ctx"), P(), P("ctx", "tp"), P("ctx", "tp"), P("ctx", "tp"),
        ),
        out_specs=P("ctx", "tp"),
        check_vma=False,
    )
```

```python
import functools

import jax
import jax.numpy as jnp
import numpy as np
from jax import lax
from jax.experimental import pallas as pl
from jax.experimental.pallas import tpu as pltpu
from jax.sharding import PartitionSpec as P

HEAD = 128
ROPE_BASE = 500000.0
MESH = pl.DeviceIdType.MESH
F32 = jnp.float32
BF16 = jnp.bfloat16
NZ, NX = 8, 4
NCTX = 64
CAP = 4
WB = 384
KB = 272
NQ = 2
KQ = 2
NEAR = (1, 2, 3, 5)
PLAN = (4, 5, 7, 8)
TWIN = (4, 5, 7, 8)
FAR = (6, 7, 8, 9)
WPASS = (1, 2, 4, 6)
WDONE = (8, 8, 9, 10)
KPASS = (2, 3, 5, 7)
KDONE = (4, 5, 8, 9)
QMID = (3, 4, 7, 8)
QGOT = (5, 6, 9, 10)
ATT = (5, 6, 9, 10)
ORDER = (
    (0, 1, 2, 3, 4, 5, 6, 7),
    (1, 0, 2, 3, 4, 5, 6, 7),
    (2, 3, 1, 4, 0, 5, 6, 7),
    (3, 4, 2, 5, 1, 6, 7, 0),
)


def dot(a, b):
    return jnp.dot(a, b, preferred_element_type=F32)


def iota(shape, dim):
    return lax.broadcasted_iota(jnp.int32, shape, dim)


def plane_at(z, i):
    low = jnp.minimum(z, NZ - 1 - z)
    packed = [sum(p << (3 * n) for n, p in enumerate(row)) for row in ORDER]
    code = jnp.where(
        low < 2,
        jnp.where(low == 0, packed[0], packed[1]),
        jnp.where(low == 2, packed[2], packed[3]),
    )
    plane = (code >> (3 * i)) % NZ
    return jnp.where(z < NZ // 2, plane, NZ - 1 - plane)


class Gather:
    def __init__(self, buf, rows, n, sems, place):
        cut = [rows // 16 * q // n * 16 for q in range(n + 1)]
        self.buf, self.n = buf, n
        self.chunks = [(a, b - a) for a, b in zip(cut, cut[1:])]
        self.zs, self.zr, self.gs, self.xs, self.xr, self.fs, self.fr = sems
        self.z, self.x, self.core = place
        self.gate = jnp.where(self.z < NZ // 2, NZ // 2, NZ // 2 - 1)

    def copy(self, plane, x, q, send, recv, z, to_x):
        start, size = self.chunks[q]
        ref = self.buf.at[plane, x, pl.ds(start, size)]
        return pltpu.make_async_remote_copy(
            src_ref=ref,
            dst_ref=ref,
            send_sem=send,
            recv_sem=recv,
            device_id={"ctx": z * 8 + to_x * 2 + self.core},
            device_id_type=MESH,
        )

    def along_z(self, plane, q, step):
        k = 0 if step > 0 else 1
        return self.copy(
            plane, self.x, q, self.zs.at[plane, q, k], self.zr.at[plane, q], self.z + step, self.x
        )

    def to_gate(self, q):
        return self.copy(
            self.z, self.x, q, self.gs.at[q], self.zr.at[self.z, q], self.gate, self.x
        )

    def goes(self, plane, step):
        if step > 0:
            return (plane <= self.z) & (self.z % (NZ // 2) < NZ // 2 - 1)
        return (plane >= self.z) & (self.z % (NZ // 2) > 0)

    def along_x(self, plane, q, k):
        to_x = (self.x + (1 if k == 0 else 3)) % NX
        return self.copy(
            plane, self.x, q, self.xs.at[plane, q, k], self.xr.at[plane, q, k], self.z, to_x
        )

    def came_x(self, plane, q, k):
        from_x = (self.x + (3 if k == 0 else 1)) % NX
        return self.copy(
            plane, from_x, q, self.xs.at[plane, q, k], self.xr.at[plane, q, k], self.z, from_x
        )

    def turn(self, q):
        return 0 if q < self.n // 2 else 1

    def onward(self, plane, q):
        k = self.turn(q)
        block_x = (self.x + (3 if k == 0 else 1)) % NX
        to_x = (self.x + (1 if k == 0 else 3)) % NX
        return self.copy(
            plane, block_x, q, self.fs.at[plane, q], self.fr.at[plane, q], self.z, to_x
        )

    def came_onward(self, plane, q):
        far_x = (self.x + 2) % NX
        return self.copy(
            plane, far_x, q, self.fs.at[plane, q], self.fr.at[plane, q], self.z, far_x
        )

    def source(self, q):
        self.to_gate(q).start()
        self.spread(self.z, q)

    def spread(self, plane, q):
        for step in (1, -1):

            @pl.when(self.goes(plane, step))
            def _():
                self.along_z(plane, q, step).start()

        self.along_x(plane, q, 0).start()
        self.along_x(plane, q, 1).start()

    def arrive(self, plane):
        for q in range(self.n):
            self.copy(
                plane, self.x, q, self.zs.at[plane, q, 0], self.zr.at[plane, q], self.z, self.x
            ).wait_recv()
            self.spread(plane, q)

    def pass_on(self, plane):
        for q in range(self.n):
            self.came_x(plane, q, self.turn(q)).wait_recv()
            self.onward(plane, q).start()

    def complete(self, plane):
        for q in range(self.n):
            self.came_x(plane, q, 1 - self.turn(q)).wait_recv()
        for q in range(self.n):
            self.came_onward(plane, q).wait_recv()

    def drain(self):
        for q in range(self.n):
            self.to_gate(q).wait_send()

        @pl.loop(0, NZ)
        def _(plane):
            for q in range(self.n):
                for step in (1, -1):

                    @pl.when(self.goes(plane, step))
                    def _():
                        self.along_z(plane, q, step).wait_send()

                self.along_x(plane, q, 0).wait_send()
                self.along_x(plane, q, 1).wait_send()
                self.onward(plane, q).wait_send()


def kernel(
    stored, owner_ref, doc_ref, starts_ref, freq_ref, wq, wk, wv, out,
    meta, table, wg, xa, acc, cosine, sine, select, unpack, pos_doc, q_doc,
    outgoing, middle, incoming, kv, qp, top, total, summed, scores,
    table_send, table_recv, own_sems, swap_send, swap_recv, act_send, act_recv,
    wzs, wzr, wgs, wxs, wxr, wfs, wfr,
    kzs, kzr, kgs, kxs, kxr, kfs, kfr,
    sib_send, sib_recv, q_send, q_recv,
):
    c = lax.axis_index("ctx")
    t = lax.axis_index("tp")
    z, x, core = c // 8, (c // 2) % NX, c % 2
    y, zh = t // 2, t % 2
    chip = c // 2
    cell = c % 8
    sib = chip * 2 + (1 - core)
    place = (z, x, core)
    first = core == 0
    weights = Gather(wg, WB, NQ, (wzs, wzr, wgs, wxs, wxr, wfs, wfr), place)
    keyvals = Gather(kv.at[core], KB, KQ, (kzs, kzr, kgs, kxs, kxr, kfs, kfr), place)

    def on_line(i):
        return ((z + i) % NZ) * 8 + cell

    def in_plane(i):
        return z * 8 + (cell + i) % 8

    def own_copies(w_third):
        refs = [wq.at[:, pl.ds(pl.multiple_of((core * 2 + g) * HEAD, HEAD), HEAD)] for g in range(2)]
        return [
            pltpu.make_async_copy(
                ref,
                wg.at[z, x, pl.ds(pl.multiple_of(core * 192 + g * 64, 64), 64)],
                own_sems.at[g],
            )
            for g, ref in enumerate(refs + [w_third])
        ]

    def swap_copies(w_third, mine):
        low = (1 - core) * 2
        refs = [wq.at[:, pl.ds(pl.multiple_of((low + g) * HEAD, HEAD), HEAD)] for g in range(2)]
        row = core if mine else 1 - core
        return [
            pltpu.make_async_remote_copy(
                src_ref=ref,
                dst_ref=wg.at[z, x, pl.ds(pl.multiple_of(row * 192 + g * 64, 64), 64)],
                send_sem=swap_send.at[g],
                recv_sem=swap_recv.at[g],
                device_id={"ctx": sib},
                device_id_type=MESH,
            )
            for g, ref in enumerate(refs + [w_third])
        ]

    own_acts_copy = pltpu.make_async_copy(stored, xa.at[t, core], own_sems.at[3])
    own_acts_copy.start()

    @pl.when(first)
    def _():
        for one in own_copies(wk):
            one.start()

    @pl.when(jnp.logical_not(first))
    def _():
        for one in own_copies(wv):
            one.start()

    meta[0:1, :] = owner_ref[...]
    meta[1:2, :] = doc_ref[...]

    barrier = pltpu.get_barrier_semaphore()

    @pl.loop(1, 8)
    def _(i):
        for to in (on_line(i), in_plane(i)):
            pl.semaphore_signal(barrier, inc=1, device_id={"ctx": to}, device_id_type=MESH)

    def y_peer(step):
        return ((y + step) % 4) * 2 + zh

    twin = y * 2 + (1 - zh)
    for to in (y_peer(1), y_peer(2), y_peer(3), twin):
        pl.semaphore_signal(barrier, inc=1, device_id={"tp": to}, device_id_type=MESH)
    pl.semaphore_wait(barrier, 7 + 7 + 4)

    @pl.when(first)
    def _():
        for one in swap_copies(wv, True):
            one.start()

    @pl.when(jnp.logical_not(first))
    def _():
        for one in swap_copies(wk, True):
            one.start()

    for one in own_copies(wk):
        one.wait()

    def source_half(which):
        for q in range(NQ // 2):
            weights.source(which * (NQ // 2) + q)

    @pl.when(first)
    def _():
        source_half(0)

    @pl.when(jnp.logical_not(first))
    def _():
        source_half(1)

    def act(src, slot, k, axis, to):
        return pltpu.make_async_remote_copy(
            src_ref=src,
            dst_ref=xa.at[slot, core],
            send_sem=act_send.at[k],
            recv_sem=act_recv.at[slot, core],
            device_id={axis: to},
            device_id_type=MESH,
        )

    def act_wait(slot, who):
        pltpu.make_async_remote_copy(
            src_ref=xa.at[slot, who],
            dst_ref=xa.at[slot, who],
            send_sem=act_send.at[0],
            recv_sem=act_recv.at[slot, who],
            device_id={"tp": t},
            device_id_type=MESH,
        ).wait_recv()

    own_acts = [act(stored, t, 0, "tp", twin)]
    own_acts += [act(stored, t, k, "tp", y_peer(k)) for k in (1, 3, 2)]
    own_acts += [act(stored, t, 4, "ctx", sib)]
    for one in own_acts:
        one.start()
    twin_acts = [act(xa.at[twin, core], twin, 4 + k, "tp", y_peer(k)) for k in (1, 3, 2)]
    twin_acts += [act(xa.at[twin, core], twin, 8, "ctx", sib)]
    across = [
        act(xa.at[y_peer(k), core], y_peer(k), 8 + k, "ctx", sib) for k in (1, 2, 3)
    ]
    across_twin = [
        act(xa.at[(y_peer(k) // 2) * 2 + (1 - zh), core], (y_peer(k) // 2) * 2 + (1 - zh), 11 + k, "ctx", sib)
        for k in (1, 2, 3)
    ]

    for one in swap_copies(wk, False):
        one.wait_recv()

    @pl.when(first)
    def _():
        source_half(1)

    @pl.when(jnp.logical_not(first))
    def _():
        source_half(0)

    def table_near(to):
        return pltpu.make_async_remote_copy(
            src_ref=meta,
            dst_ref=table.at[c],
            send_sem=table_send.at[0],
            recv_sem=table_recv.at[0],
            device_id={"ctx": to},
            device_id_type=MESH,
        )

    def table_far(to):
        ref = table.at[pl.ds(z * 8, 8)]
        return pltpu.make_async_remote_copy(
            src_ref=ref,
            dst_ref=ref,
            send_sem=table_send.at[1],
            recv_sem=table_recv.at[1],
            device_id={"ctx": to},
            device_id_type=MESH,
        )

    @pl.loop(1, 8)
    def _(i):
        table_near(in_plane(i)).start()

    pltpu.make_async_copy(meta, table.at[c], table_recv.at[0]).start()

    def table_onward():
        ref = table.at[pl.ds(z * 8, 8)]
        pltpu.make_async_copy(ref, ref, table_recv.at[0]).wait()

        @pl.loop(1, NZ)
        def _(i):
            table_far(on_line(i)).start()

    def plan():
        far = table.at[pl.ds(0, 56)]
        pltpu.make_async_copy(far, far, table_recv.at[1]).wait()
        owners = table[:, 0, :]
        docs = table[:, 1, :].astype(F32).astype(BF16)
        before_l = (iota((128, 128), 0) < iota((128, 128), 1)).astype(F32).astype(BF16)
        before_s = (iota((64, 64), 1) < iota((64, 64), 0)).astype(F32).astype(BF16)
        rows = iota((512, 128), 0)
        spread_rows = (iota((512, 64), 0) // 8 == iota((512, 64), 1)).astype(F32).astype(BF16)
        doc_tile = jnp.zeros((16, 128), F32)
        for oc in range(2):
            hit = owners == chip * 2 + oc
            hot = hit.astype(F32)
            hot16 = hot.astype(BF16)
            lane_before = dot(hot16, before_l)
            count = jnp.broadcast_to(jnp.sum(hot, axis=1, keepdims=True), (64, 128))
            before = jnp.broadcast_to(
                jnp.sum(dot(before_s, hot16), axis=1, keepdims=True), (64, 128)
            )
            rank1 = jnp.where(hit, before + lane_before + 1.0, 0.0)
            before_t = jnp.concatenate([before, before], axis=0).T[:, :64]
            count_t = jnp.concatenate([count, count], axis=0).T[:, :64]
            r64 = iota((128, 64), 0).astype(F32)
            shard_hot = jnp.where((before_t <= r64) & (r64 < before_t + count_t), 1.0, 0.0)
            shard_hot16 = shard_hot.astype(BF16)
            ranks = dot(shard_hot16, rank1.astype(BF16))
            found = ranks == iota((128, 128), 0).astype(F32) + 1.0
            lane = jnp.sum(
                jnp.where(found, iota((128, 128), 1).astype(F32), 0.0), axis=1, keepdims=True
            )
            doc = jnp.sum(
                jnp.where(found, dot(shard_hot16, docs), 0.0), axis=1, keepdims=True
            )
            shard = jnp.sum(
                shard_hot * iota((128, 64), 1).astype(F32), axis=1, keepdims=True
            )
            n_doc = starts_ref.shape[1]
            starts = jnp.broadcast_to(starts_ref[...].astype(F32), (128, n_doc))
            start = jnp.sum(
                jnp.where(doc == iota((128, n_doc), 1).astype(F32), starts, 0.0),
                axis=1,
                keepdims=True,
            )
            position = shard * 128.0 + lane - start
            angle = position * freq_ref[...]
            span = pl.ds(oc * 128, 128)
            cosine[span, :] = jnp.cos(angle)
            sign = jnp.where(iota((128, 128), 1) < 64, -1.0, 1.0)
            sine[span, :] = jnp.sin(angle) * sign
            doc_rows = jnp.broadcast_to(doc, (128, 128)).T
            doc_tile = jnp.where(iota((16, 128), 0) == oc, doc_rows[:16], doc_tile)
            begin = dot(spread_rows, before.astype(BF16))
            many = dot(spread_rows, count.astype(BF16))
            slot = (rows % CAP).astype(F32)
            chosen = (
                (iota((512, 128), 1).astype(F32) == begin + slot)
                & (slot < many)
                & ((rows // CAP) % 2 == oc)
            )
            select[:, oc * 128 : (oc + 1) * 128] = jnp.where(chosen, 1.0, 0.0).astype(BF16)
        pos_doc[...] = doc_tile.astype(BF16)
        mine = jnp.broadcast_to(owner_ref[...].astype(F32), (128, 128))
        mine_t = mine.T
        same = (mine == mine_t) & (iota((128, 128), 1) < iota((128, 128), 0))
        order = jnp.sum(jnp.where(same, 1.0, 0.0), axis=1, keepdims=True)
        col = iota((128, 512), 1)
        chip_col = (col // 16 % NZ) * NX + col // 128
        owner_col = (chip_col * 2 + (col // CAP) % 2).astype(F32)
        slot_col = (col % CAP).astype(F32)
        mine_col = jnp.broadcast_to(mine_t[:, :1], (128, 512))
        for hd in range(2):
            pick = (owner_col == mine_col) & (slot_col == order) & ((col // 8) % 2 == hd)
            unpack[hd] = jnp.where(pick, 1.0, 0.0).astype(BF16)
        q_doc[...] = jnp.broadcast_to(doc_ref[...].astype(F32), (128, 128)).T

    def project(plane):
        columns = []
        for xx in range(NX):
            for half_core in range(2):
                tiles = [
                    wg[plane, xx, half_core * 192 + g * 64 : half_core * 192 + (g + 1) * 64, :]
                    for g in range(3)
                ]
                columns.append(jnp.concatenate(tiles, axis=1))
        w = jnp.concatenate(columns, axis=0)
        acts = xa[plane].reshape(256, 512)
        acc[...] += dot(acts, w)

    acc[...] = jnp.zeros_like(acc)
    top[...] = jnp.full_like(top, -1e30)
    total[...] = jnp.zeros_like(total)
    summed[...] = jnp.zeros_like(summed)

    low = jnp.minimum(z, NZ - 1 - z)

    def when(row):
        return jnp.where(
            low < 2, jnp.where(low == 0, row[0], row[1]), jnp.where(low == 2, row[2], row[3])
        )

    def each(i, row, go):
        begin = when(row)

        @pl.when((i >= begin) & (i < begin + NZ))
        def _():
            go(plane_at(z, i - begin))

    def once(i, row, go):
        @pl.when(i == when(row))
        def _():
            go()

    def acts_near():
        for k in (1, 2, 3):
            act_wait(y_peer(k), core)
            across[k - 1].start()

    def acts_twin():
        act_wait(twin, core)
        for one in twin_acts:
            one.start()

    def acts_far():
        for k in (1, 2, 3):
            act_wait((y_peer(k) // 2) * 2 + (1 - zh), core)
            across_twin[k - 1].start()

    def all_acts():
        own_acts_copy.wait()

        @pl.loop(0, 8)
        def _(slot):
            act_wait(slot, 1 - core)

    def use_plane(plane):
        weights.complete(plane)
        project(plane)

    @pl.loop(0, NZ + max(WDONE))
    def _(i):
        @pl.when((i > 0) & (i < NZ))
        def _():
            weights.arrive(plane_at(z, i))

        once(i, (1, 1, 1, 1), table_onward)
        once(i, NEAR, acts_near)
        once(i, TWIN, acts_twin)
        once(i, PLAN, plan)
        once(i, FAR, acts_far)
        each(i, WPASS, weights.pass_on)
        once(i, WDONE, all_acts)
        each(i, WDONE, use_plane)

    def rotate(v):
        return v * cosine[...] + pltpu.roll(v, 64, 1) * sine[...]

    third = acc[:, 256:384]
    kv[core, z, x, 0:256, :] = jnp.where(first, rotate(third), third).astype(BF16)
    kv[core, z, x, 256:272, :] = pos_doc[...]
    for q in range(KQ):
        keyvals.source(q)
    blocks = []
    for hd in range(2):
        rotated = rotate(acc[:, hd * HEAD : (hd + 1) * HEAD]).astype(BF16)
        blocks.append(dot(select[...], rotated).reshape(64, 8, HEAD))
    outgoing[...] = jnp.concatenate(blocks, axis=1).astype(BF16)

    def q_far(i):
        return pltpu.make_async_remote_copy(
            src_ref=outgoing.at[pl.ds(((z + i) % NZ) * 8, 8)],
            dst_ref=middle.at[z],
            send_sem=q_send.at[0],
            recv_sem=q_recv.at[0],
            device_id={"ctx": on_line(i)},
            device_id_type=MESH,
        )

    def q_near(i):
        return pltpu.make_async_remote_copy(
            src_ref=middle.at[:, (cell + i) % 8],
            dst_ref=incoming.at[core, x],
            send_sem=q_send.at[1],
            recv_sem=q_recv.at[1],
            device_id={"ctx": in_plane(i)},
            device_id_type=MESH,
        )

    @pl.loop(1, NZ)
    def _(i):
        q_far(i).start()

    pltpu.make_async_copy(outgoing.at[pl.ds(z * 8, 8)], middle.at[z], q_recv.at[0]).start()

    def q_onward():
        pltpu.make_async_copy(middle, middle, q_recv.at[0]).wait()

        @pl.loop(1, 8)
        def _(i):
            q_near(i).start()

        pltpu.make_async_copy(middle.at[:, cell], incoming.at[core, x], q_recv.at[1]).start()

    def sibling(plane, who):
        return pltpu.make_async_remote_copy(
            src_ref=kv.at[who, plane],
            dst_ref=kv.at[who, plane],
            send_sem=sib_send.at[plane],
            recv_sem=sib_recv.at[plane],
            device_id={"ctx": sib},
            device_id_type=MESH,
        )

    factor2 = 1.4426950408889634 / HEAD**0.5

    def collect():
        pltpu.make_async_copy(incoming, incoming, q_recv.at[1]).wait()
        for who in range(2):
            block = incoming[who].reshape(512, HEAD)
            for hd in range(2):
                qp[who * 2 + hd] = dot(unpack[hd], block).astype(BF16)

    def masked_scores(plane, h0, key_doc):
        q = qp[h0 : h0 + 2].reshape(256, HEAD)
        query_doc = jnp.concatenate([q_doc[...]] * 2, axis=1)
        largest = None
        for xx in range(NX):
            block = lax.dot_general(
                q,
                kv[0, plane, xx, 0:256, :],
                (((1,), (1,)), ((), ())),
                preferred_element_type=F32,
            )
            kept = query_doc == key_doc[xx]
            block = jnp.where(jnp.concatenate([kept] * 2, axis=0), block * factor2, -2e30)
            scores[h0 * HEAD : h0 * HEAD + 256, xx * 256 : (xx + 1) * 256] = block
            here = jnp.maximum(block[:, :HEAD], block[:, HEAD:])
            largest = here if largest is None else jnp.maximum(largest, here)
        return largest

    def weigh(plane, h0, largest):
        two = slice(h0, h0 + 2)
        old = top[two].reshape(256, HEAD)
        new = jnp.maximum(old, jnp.max(largest, axis=1, keepdims=True))
        fall = jnp.exp2(old - new)
        lanes = total[two].reshape(256, HEAD) * fall
        mixed = summed[two].reshape(256, HEAD) * fall
        wide = jnp.concatenate([new, new], axis=1)
        for xx in range(NX):
            block = scores[h0 * HEAD : h0 * HEAD + 256, xx * 256 : (xx + 1) * 256]
            block = jnp.exp2(block - wide)
            lanes = lanes + (block[:, :HEAD] + block[:, HEAD:])
            mixed = mixed + dot(block.astype(BF16), kv[1, plane, xx, 0:256, :])
        total[two] = lanes.reshape(2, 128, HEAD)
        summed[two] = mixed.reshape(2, 128, HEAD)
        top[two] = new.reshape(2, 128, HEAD)

    def attend(plane):
        key_doc = []
        for xx in range(NX):
            tile = kv[0, plane, xx, 256:272, :].astype(F32)
            key_doc.append(jnp.concatenate([tile[0:1, :], tile[1:2, :]], axis=1))
        one = masked_scores(plane, 0, key_doc)
        two = masked_scores(plane, 2, key_doc)
        weigh(plane, 0, one)
        weigh(plane, 2, two)

    def finish_plane(plane):
        keyvals.complete(plane)
        sibling(plane, core).start()

    def attend_plane(plane):
        sibling(plane, 1 - core).wait_recv()
        attend(plane)

    @pl.loop(0, NZ + max(ATT))
    def _(i):
        @pl.when((i > 0) & (i < NZ))
        def _():
            keyvals.arrive(plane_at(z, i))

        each(i, KPASS, keyvals.pass_on)
        once(i, QMID, q_onward)
        each(i, KDONE, finish_plane)
        once(i, QGOT, collect)
        each(i, ATT, attend_plane)

    for h in range(4):
        whole = jnp.sum(total[h], axis=1, keepdims=True)
        out[:, h * HEAD : (h + 1) * HEAD] = (summed[h] / whole).astype(BF16)

    for one in swap_copies(wk, True):
        one.wait_send()
    for one in own_acts + twin_acts + across + across_twin:
        one.wait_send()
    weights.drain()
    keyvals.drain()

    @pl.loop(0, NZ)
    def _(plane):
        sibling(plane, core).wait_send()

    near = table.at[pl.ds(0, 7)]
    pltpu.make_async_copy(near, near, table_send.at[0]).wait()
    far = table.at[pl.ds(0, 56)]
    pltpu.make_async_copy(far, far, table_send.at[1]).wait()
    for k in range(2):
        pltpu.make_async_copy(
            middle.at[pl.ds(0, 7)], middle.at[pl.ds(0, 7)], q_send.at[k]
        ).wait()


def body(stored, source_owner, doc_ids, doc_starts, wq, wk, wv):
    half = HEAD // 2
    freqs = np.float32(ROPE_BASE) ** (-np.arange(half, dtype=np.float32) * np.float32(2.0 / HEAD))
    freqs = jnp.asarray(np.concatenate([freqs, freqs])[None, :], F32)
    dma = pltpu.SemaphoreType.DMA

    def ring_sems(n):
        shapes = ((NZ, n, 2), (NZ, n), (n,), (NZ, n, 2), (NZ, n, 2), (NZ, n), (NZ, n))
        return [dma(shape) for shape in shapes]

    scratch = [
        pltpu.VMEM((2, 128), jnp.int32),
        pltpu.VMEM((NCTX, 2, 128), jnp.int32),
        pltpu.VMEM((NZ, NX, WB, HEAD), BF16),
        pltpu.VMEM((8, 2, 128, 512), BF16),
        pltpu.VMEM((256, 384), F32),
        pltpu.VMEM((256, HEAD), F32),
        pltpu.VMEM((256, HEAD), F32),
        pltpu.VMEM((512, 256), BF16),
        pltpu.VMEM((2, 128, 512), BF16),
        pltpu.VMEM((16, 128), BF16),
        pltpu.VMEM((128, 128), F32),
        pltpu.VMEM((NCTX, 16, HEAD), BF16),
        pltpu.VMEM((NZ, 8, 16, HEAD), BF16),
        pltpu.VMEM((2, NX, NZ, 16, HEAD), BF16),
        pltpu.VMEM((2, NZ, NX, KB, HEAD), BF16),
        pltpu.VMEM((4, 128, HEAD), BF16),
        pltpu.VMEM((4, 128, HEAD), F32),
        pltpu.VMEM((4, 128, HEAD), F32),
        pltpu.VMEM((4, 128, HEAD), F32),
        pltpu.VMEM((512, 1024), F32),
        dma((2,)), dma((2,)), dma((4,)), dma((3,)), dma((3,)), dma((15,)), dma((8, 2)),
        *ring_sems(NQ),
        *ring_sems(KQ),
        dma((NZ,)), dma((NZ,)), dma((2,)), dma((2,)),
    ]
    vmem = pl.BlockSpec(memory_space=pltpu.VMEM)
    hbm = pl.BlockSpec(memory_space=pltpu.HBM)
    return pl.pallas_call(
        kernel,
        out_shape=jax.ShapeDtypeStruct((128, 512), BF16),
        in_specs=[hbm] + [vmem] * 4 + [hbm] * 3,
        out_specs=vmem,
        scratch_shapes=scratch,
        compiler_params=pltpu.CompilerParams(
            collective_id=0, has_side_effects=True, vmem_limit_bytes=62 << 20
        ),
        name="layer",
    )(stored, source_owner[None, :], doc_ids[None, :], doc_starts[None, :], freqs, wq, wk, wv)


def solution(mesh):
    return jax.shard_map(
        body,
        mesh=mesh,
        in_specs=(
            P("ctx", "tp"), P("ctx"), P("ctx"), P(), P("ctx", "tp"), P("ctx", "tp"), P("ctx", "tp"),
        ),
        out_specs=P("ctx", "tp"),
        check_vma=False,
    )
```
